1024 devices in a mesh: grp: 8 (over z_lo), blk: 128 (over x, z_hi, y, core).
Axes of the slice: x: 4, y: 8, z: 16 (z_hi: 2, z_lo: 8; z = z_hi * 8 + z_lo), core: 2. Of those that a mesh axis runs over, the one named last changes fastest.
Arguments:
- velocity_coef: float32 [2, 2, 8, 512, 512], P(None, None, 'grp', 'blk'), may hold values from -24 to 24
- scalar_field: float32 [32, 2048, 2048], P('grp', 'blk'), may hold values from -3 to 8
- plane_offset: int32 [32], P('grp'), may hold values from 0 to 127, as said below
Outputs:
- velocity_next: float32 [2, 2, 8, 512, 512], P(None, None, 'grp', 'blk')
- scalar_next: float32 [32, 2048, 2048], P('grp', 'blk')
The draws below stay inside these ranges and needn't reach their ends.
Inputs may be any that keep to these rules, and one draw needn't show every extreme that they name: Fine plane n lies at z = plane_offset[n] / 16 coarse plane spacings (periodic), with 4 n <= plane_offset[n] <= 4 n + 3.
All inputs are finite; a program needn't handle non-finite values.
Results may differ from the reference program's by a relative error of at most 0.0003.
Values sent between devices are 32-bit elements; how exact they have to be, the bound alone decides.
A program may use at most 64 MiB of HBM per device.

```python
import jax
import jax.numpy as jnp
from jax import lax

NV = 512
STEPS = 1
NZC = 8
NF = 2048
NPL = 32


def draw_plane_offset(key, part):
    position = jnp.arange(NPL, dtype=jnp.int32)
    jitter = jax.random.randint(key, (NPL,), 0, 4, dtype=jnp.int32)
    jitter = jnp.where(position == 0, 0, jnp.where(position == NPL - 1, 3, jitter))
    return 4 * position + jitter


def draw_velocity_coef(key, part):
    shape = (2, 2, NZC, NV, NV)
    values = 7.0 * jax.random.truncated_normal(key, -3.4, 3.4, shape, jnp.float32)
    return values.astype(jnp.float32)


def draw_scalar_field(key, part):
    rough_key = jax.random.fold_in(key, 11)
    phase_key = jax.random.fold_in(key, 23)
    phases = jax.random.uniform(phase_key, (NPL, 2), jnp.float32, 0.0, 1.0)
    position = jnp.arange(NF, dtype=jnp.float32) / NF
    wave_x = jnp.sin(2.0 * jnp.pi * (position[None, :] + phases[:, 0:1]))
    wave_y = jnp.sin(2.0 * jnp.pi * (position[None, :] + phases[:, 1:2]))
    pattern = wave_x[:, :, None] * wave_y[:, None, :]
    rough = jax.random.truncated_normal(rough_key, -4.0, 4.0, (NPL, NF, NF), jnp.float32)
    smooth = 2.5 + 0.8 * pattern
    return (rough + smooth).astype(jnp.float32)


def setup_inputs(seed: int = 0) -> dict:
    key_of = jax.random.split(jax.random.key(seed), 4)
    velocity_coef = draw_velocity_coef(jax.random.fold_in(key_of[3], 71), 0)
    scalar_field = draw_scalar_field(jax.random.fold_in(key_of[3], 71), 0)
    plane_offset = draw_plane_offset(jax.random.fold_in(key_of[3], 71), 0)
    return {"velocity_coef": velocity_coef, "scalar_field": scalar_field, "plane_offset": plane_offset}


TIME_STEP = 0.05
VISCOSITY = 0.5
STENCIL = (0.8, -0.2, 4.0 / 105.0, -1.0 / 280.0)


def signed_waves(length):
    wave_index = jnp.arange(length, dtype=jnp.int32)
    return jnp.where(2 * wave_index < length, wave_index, wave_index - length)


def refine(values, axis_index):
    above_part = jnp.roll(values, -1, axis_index)
    length = values.shape[axis_index]
    fraction = jnp.tile(jnp.array([0.0, 0.25, 0.5, 0.75], jnp.float32), length)
    layout = [1] * values.ndim
    layout[axis_index] = 4 * length
    fraction = fraction.reshape(layout)
    return jnp.repeat(values, 4, axis_index) * (1.0 - fraction) + jnp.repeat(above_part, 4, axis_index) * fraction


def tendency(values, velocity_fine):
    along_x = 0.0
    along_y = 0.0
    for offset, weight in zip((1, 2, 3, 4), STENCIL):
        along_x = along_x + weight * (jnp.roll(values, -offset, 0) - jnp.roll(values, offset, 0))
        along_y = along_y + weight * (jnp.roll(values, -offset, 1) - jnp.roll(values, offset, 1))
    return -(velocity_fine[0] * (4.0 * along_x) + velocity_fine[1] * (4.0 * along_y))


def synthesize(complex_coef):
    return (jnp.real(jnp.fft.ifft2(complex_coef, axes=(-2, -1))) * NV).swapaxes(-1, -2)


def reference(velocity_coef, scalar_field, plane_offset):
    all_waves = signed_waves(NV)
    wavenum = all_waves.astype(jnp.float32) * (2.0 * jnp.pi / NV)
    dealias = jnp.where((3 * jnp.abs(all_waves)[:, None] < NV) & (3 * jnp.abs(all_waves)[None, :] < NV), 1.0, 0.0).astype(jnp.float32)
    damping = jnp.exp(-VISCOSITY * TIME_STEP * (wavenum[:, None] ** 2 + wavenum[None, :] ** 2))
    spectral = velocity_coef
    scalar_now = scalar_field
    for step_index in range(STEPS):
        complex_coef = spectral[:, 0] + 1j * spectral[:, 1]
        velocity = synthesize(complex_coef)
        grad_x = synthesize(complex_coef * (1j * wavenum[None, :]))
        grad_y = synthesize(complex_coef * (1j * wavenum[:, None]))
        advect = velocity[0:1] * grad_x + velocity[1:2] * grad_y
        transformed = jnp.fft.fft2(advect.swapaxes(-1, -2), axes=(-2, -1)) / NV
        spectrum = jnp.stack([jnp.real(transformed), jnp.imag(transformed)], 1) * dealias
        spectral_next = damping * (spectral - TIME_STEP * spectrum)

        def plane_update(paired):
            scalar_plane, offset_value = paired
            base_plane = offset_value // 16
            fraction = (offset_value % 16).astype(jnp.float32) * 0.0625
            next_plane = (base_plane + 1) % NZC
            plane_vel = (1.0 - fraction) * lax.dynamic_index_in_dim(velocity, base_plane, 1, keepdims=False) + fraction * lax.dynamic_index_in_dim(velocity, next_plane, 1, keepdims=False)
            fine_velocity = refine(refine(plane_vel, 1), 2)
            section_one = scalar_plane + TIME_STEP * tendency(scalar_plane, fine_velocity)
            return 0.5 * (scalar_plane + section_one + TIME_STEP * tendency(section_one, fine_velocity))

        scalar_now = lax.map(plane_update, (scalar_now, plane_offset))
        spectral = spectral_next
    return spectral, scalar_now
```

```python
import functools

import jax
import jax.numpy as jnp
import numpy as np
from jax import lax
from jax.experimental import pallas as pl
from jax.experimental.pallas import tpu as pltpu
from jax.sharding import PartitionSpec as P

TIME_STEP = 0.05
VISCOSITY = 0.5
STENCIL = (0.8, -0.2, 4.0 / 105.0, -1.0 / 280.0)
HIGHEST = lax.Precision.HIGHEST
MESH = pl.DeviceIdType.MESH
NV = 512
OUTER = 8
INNER = 16
BLOCKS = OUTER * INNER
F32 = jnp.float32


def tables():
    base = np.arange(128)
    angle = 2.0 * np.pi * ((base[:, None] * base[None, :]) % 128) / 128.0
    table = np.concatenate([np.cos(angle), np.sin(angle)], 1)
    wave = np.arange(NV)
    signed = np.where(2 * wave < NV, wave, wave - NV)
    wavenum = 2.0 * np.pi * signed / NV
    rows = np.arange(8) - 1
    ang_x = 2.0 * np.pi * ((rows[:, None] * wave[None, :]) % NV) / NV
    cos_x, sin_x = np.cos(ang_x) / NV, np.sin(ang_x) / NV
    send = np.stack([cos_x, sin_x, -wavenum * sin_x, wavenum * cos_x], 0)
    digit = np.arange(4)
    ang_d = 2.0 * np.pi * ((digit[:, None] * wave[None, :]) % NV) / NV
    turn = np.stack([np.cos(ang_d), np.sin(ang_d)], 0)
    lane_digit = (np.arange(128) // 16) % 4
    ky = 4 * base[:, None] + lane_digit[None, :]
    weight = wavenum[ky]
    as32 = lambda a: np.asarray(a, np.float32)
    return as32(table), as32(send), as32(turn), as32(weight)


def exchange(sent, passed, landed, sems, blk, grp):
    outer, inner = blk // INNER, blk % INNER

    own = pltpu.make_async_copy(sent.at[outer], passed.at[outer], sems.at[0])
    own.start()

    def first(k, carry):
        there = lax.rem(outer + k, OUTER)
        pltpu.make_async_remote_copy(
            sent.at[there], passed.at[outer], sems.at[1], sems.at[2],
            device_id=(grp, there * INNER + inner), device_id_type=MESH,
        ).start()
        return carry

    lax.fori_loop(1, OUTER, first, 0)

    def rest():
        some = pl.ds(0, OUTER - 1)
        every = pltpu.make_async_remote_copy(
            sent.at[some], passed.at[some], sems.at[1], sems.at[2],
            device_id=(grp, lax.rem(outer + 1, OUTER) * INNER + inner), device_id_type=MESH,
        )
        own.wait()
        every.wait_recv()
        mine = pltpu.make_async_copy(passed.at[:, inner], landed.at[:, inner], sems.at[3])
        mine.start()

        def second(k, carry):
            there = lax.rem(inner + k, INNER)
            pltpu.make_async_remote_copy(
                passed.at[:, there], landed.at[:, inner], sems.at[4], sems.at[5],
                device_id=(grp, outer * INNER + there), device_id_type=MESH,
            ).start()
            return carry

        lax.fori_loop(1, INNER, second, 0)
        every.wait_send()

        def finish():
            part = pl.ds(0, INNER - 1)
            whole = pltpu.make_async_remote_copy(
                passed.at[:, part], landed.at[:, part], sems.at[4], sems.at[5],
                device_id=(grp, outer * INNER + lax.rem(inner + 1, INNER)), device_id_type=MESH,
            )
            mine.wait()
            whole.wait_recv()
            whole.wait_send()

        return finish

    return rest


def spectral_kernel(
    coef, scalar, table, send, turn, weight,
    next_coef, velocity, above, low, high,
    pack, sent, passed, landed, pack2, sent2, passed2, landed2,
    sems, sems2, halo_sems, grp_sems,
):
    blk = lax.axis_index("blk")
    grp = lax.axis_index("grp")
    outer, inner = blk // INNER, blk % INNER
    behind, ahead = lax.rem(blk + BLOCKS - 1, BLOCKS), lax.rem(blk + 1, BLOCKS)
    groups = lax.axis_size("grp")
    below, upper = lax.rem(grp + groups - 1, groups), lax.rem(grp + 1, groups)

    barrier = pltpu.get_barrier_semaphore()

    def hello(device):
        pl.semaphore_signal(barrier, inc=1, device_id=device, device_id_type=MESH)

    def greet_outer(k, carry):
        hello((grp, lax.rem(outer + k, OUTER) * INNER + inner))
        return carry

    def greet_inner(k, carry):
        hello((grp, outer * INNER + lax.rem(inner + k, INNER)))
        return carry

    lax.fori_loop(1, OUTER, greet_outer, 0)
    lax.fori_loop(1, INNER, greet_inner, 0)
    hello((grp, behind))
    hello((grp, ahead))
    hello((upper, blk))

    real = jnp.concatenate([coef[0, 0, 0], coef[1, 0, 0]], 0)
    imag = jnp.concatenate([coef[0, 1, 0], coef[1, 1, 0]], 0)
    for row in range(8):
        for kind in range(2):
            re, im = 0.0, 0.0
            for digit in range(4):
                lanes = slice(128 * digit, 128 * digit + 128)
                tr = send[2 * kind, row : row + 1, lanes]
                ti = send[2 * kind + 1, row : row + 1, lanes]
                re = re + (tr * real[:, lanes] - ti * imag[:, lanes])
                im = im + (tr * imag[:, lanes] + ti * real[:, lanes])
            start = 128 * kind + row
            pack[0, pl.ds(start, 8, 16), :] = re
            pack[1, pl.ds(start, 8, 16), :] = -im
            pack[0, pl.ds(start + 8, 8, 16), :] = im
            pack[1, pl.ds(start + 8, 8, 16), :] = re
    along_x = lax.dot_general(
        table[...], jnp.concatenate([pack[0], pack[1]], 1), (((1,), (1,)), ((), ())), precision=HIGHEST,
        preferred_element_type=F32,
    )
    for part in range(OUTER):
        rows = slice(part * INNER, part * INNER + INNER)
        sent[part, :, 0, :] = along_x[rows, 0:128]
        sent[part, :, 1, :] = along_x[rows, 128:256]

    pl.semaphore_wait(barrier, OUTER - 1 + INNER - 1 + 3)

    step = exchange(sent, passed, landed, sems, blk, grp)
    halos = []
    for plane in range(4):
        halos.append(pltpu.make_async_remote_copy(
            scalar.at[plane, pl.ds(8, 8)], low.at[plane],
            halo_sems.at[0, plane], halo_sems.at[1, plane],
            device_id=(grp, ahead), device_id_type=MESH,
        ))
        halos.append(pltpu.make_async_remote_copy(
            scalar.at[plane, pl.ds(0, 8)], high.at[plane],
            halo_sems.at[2, plane], halo_sems.at[3, plane],
            device_id=(grp, behind), device_id_type=MESH,
        ))
    for copy in halos:
        copy.start()
    step()()

    vel_in = jnp.concatenate([landed[part, :, 0, :] for part in range(OUTER)], 0)
    der_in = jnp.concatenate([landed[part, :, 1, :] for part in range(OUTER)], 0)
    stacked = jnp.concatenate([vel_in.T, (vel_in * weight[...]).T, der_in.T], 0)
    along_y = jnp.dot(stacked, table[...], precision=HIGHEST, preferred_element_type=F32)

    def synthesize(kind, component):
        parts = [0.0] * 4
        for digit in range(4):
            start = 128 * kind + (component * 4 + digit) * 16
            cos_re = along_y[start : start + 8, 0:128]
            sin_re = along_y[start : start + 8, 128:256]
            cos_im = along_y[start + 8 : start + 16, 0:128]
            sin_im = along_y[start + 8 : start + 16, 128:256]
            if kind == 1:
                head_re, head_im = -cos_im - sin_re, cos_re - sin_im
            else:
                head_re, head_im = cos_re - sin_im, sin_re + cos_im
            for part in range(4):
                lanes = slice(128 * part, 128 * part + 128)
                tr = turn[0, digit : digit + 1, lanes]
                ti = turn[1, digit : digit + 1, lanes]
                parts[part] = parts[part] + (tr * head_re - ti * head_im)
        return parts

    vel = [synthesize(0, 0), synthesize(0, 1)]
    for component in range(2):
        for part in range(4):
            velocity[component, :, 128 * part : 128 * part + 128] = vel[component][part]
    lift = pltpu.make_async_remote_copy(
        velocity, above, grp_sems.at[0], grp_sems.at[1],
        device_id=(below, blk), device_id_type=MESH,
    )
    lift.start()

    for component in range(2):
        grad_y = synthesize(1, component)
        grad_x = synthesize(2, component)
        adv = [vel[0][a] * grad_x[a] + vel[1][a] * grad_y[a] for a in range(4)]
        even, odd = adv[0] + adv[2], adv[1] + adv[3]
        even_d, odd_d = adv[0] - adv[2], adv[1] - adv[3]
        heads = [(even + odd, None), (even_d, -odd_d), (even - odd, None), (even_d, odd_d)]
        for digit, (p, q) in enumerate(heads):
            tr = turn[0, digit : digit + 1, 0:128]
            ti = turn[1, digit : digit + 1, 0:128]
            if q is None:
                re, im = p * tr, -(p * ti)
            else:
                re, im = p * tr + q * ti, q * tr - p * ti
            start = component * 4 + digit
            pack2[0, pl.ds(start, 8, 16), :] = re
            pack2[1, pl.ds(start, 8, 16), :] = im
            pack2[0, pl.ds(start + 8, 8, 16), :] = im
            pack2[1, pl.ds(start + 8, 8, 16), :] = -re
    forward_y = lax.dot_general(
        table[...], jnp.concatenate([pack2[0], pack2[1]], 1), (((1,), (1,)), ((), ())), precision=HIGHEST,
        preferred_element_type=F32,
    )
    for part in range(OUTER):
        sent2[part, :, 0, :] = forward_y[part * INNER : part * INNER + INNER]
    exchange(sent2, passed2, landed2, sems2, blk, grp)()()

    back = jnp.concatenate([landed2[part, :, 0, :] for part in range(OUTER)], 0)
    along = jnp.dot(back.T, table[...], precision=HIGHEST, preferred_element_type=F32)
    heads = []
    for row in range(1, 5):
        start = row * 16
        cos_re = along[start : start + 8, 0:128]
        sin_re = along[start : start + 8, 128:256]
        cos_im = along[start + 8 : start + 16, 0:128]
        sin_im = along[start + 8 : start + 16, 128:256]
        heads.append((cos_re + sin_im, cos_im - sin_re))
    row_index = lax.broadcasted_iota(jnp.int32, (8, 128), 0) % 4 + blk * 4
    row_signed = jnp.where(2 * row_index < NV, row_index, row_index - NV)
    row_wave = row_signed.astype(F32) * (2.0 * np.pi / NV)
    lane = lax.broadcasted_iota(jnp.int32, (8, 128), 1)
    for part in range(4):
        lanes = slice(128 * part, 128 * part + 128)
        re, im = 0.0, 0.0
        for digit, (head_re, head_im) in enumerate(heads):
            tr = turn[0, digit : digit + 1, lanes]
            ti = turn[1, digit : digit + 1, lanes]
            re = re + (tr * head_re + ti * head_im)
            im = im + (tr * head_im - ti * head_re)
        column = lane + 128 * part
        column_signed = column if part < 2 else column - NV
        column_wave = column_signed.astype(F32) * (2.0 * np.pi / NV)
        keep = (3 * jnp.abs(row_signed) < NV) & (3 * jnp.abs(column_signed) < NV)
        gain = jnp.where(keep, TIME_STEP / NV, 0.0)
        damping = jnp.exp(-VISCOSITY * TIME_STEP * (row_wave * row_wave + column_wave * column_wave))
        new_re = damping * (real[:, lanes] - gain * re)
        new_im = damping * (imag[:, lanes] - gain * im)
        for component in range(2):
            rows = slice(4 * component, 4 * component + 4)
            next_coef[component, 0, 0, :, lanes] = new_re[rows]
            next_coef[component, 1, 0, :, lanes] = new_im[rows]

    lift.wait()
    for copy in halos:
        copy.wait()


PAD = 128
NF = 2048
SPAN = 512


def transport_kernel(offset, scalar, low, high, velocity, above, spread, out, field, first, fine_y, flow):
    def place(buffer, rows, plane, value):
        buffer[plane, rows, PAD : PAD + NF] = value
        buffer[plane, rows, 0:PAD] = value[:, NF - PAD :]
        buffer[plane, rows, PAD + NF :] = value[:, :PAD]

    for plane in range(4):
        fraction = (offset[plane] % 16).astype(F32) * 0.0625
        for component in range(2):
            mixed = (1.0 - fraction) * velocity[component] + fraction * above[component]
            wide = jnp.concatenate([mixed, mixed[:, :128]], 1)
            rows = jnp.concatenate([wide[:, 128 * m : 128 * m + 256] for m in range(4)], 0)
            top = rows.astype(jnp.bfloat16)
            rest = (rows - top.astype(F32)).astype(jnp.bfloat16)
            fine_y[plane, component] = jnp.dot(
                top, spread[...], preferred_element_type=F32
            ) + jnp.dot(rest, spread[...], preferred_element_type=F32)

    index = lax.broadcasted_iota(jnp.int32, (8, 128), 0)
    share = (index % 4).astype(F32) * 0.25
    half = index < 4
    share_a = jnp.where(half, 1.0 - share, 0.0)
    share_b = jnp.where(half, share, 1.0 - share)
    share_c = jnp.where(half, 0.0, share)

    def wide_weights(value):
        return jnp.concatenate([value] * (SPAN // 128), 1)

    share_a, share_b, share_c = wide_weights(share_a), wide_weights(share_b), wide_weights(share_c)

    def along(values, axis):
        size = values.shape[axis]
        total = 0.0
        for offset_m, weight in zip((1, 2, 3, 4), STENCIL):
            total = total + (TIME_STEP * 4.0 * weight) * (
                pltpu.roll(values, size - offset_m, axis) - pltpu.roll(values, offset_m, axis)
            )
        return total

    def plane_step(plane, carry):
        place(field, slice(0, 8), plane, low[plane])
        place(field, slice(8, 24), plane, scalar[plane])
        place(field, slice(24, 32), plane, high[plane])
        for m in range(4):
            lanes = slice(SPAN * m, SPAN * m + SPAN)
            window = field[plane, :, SPAN * m : SPAN * m + SPAN + 2 * PAD]
            center = window[:, PAD : PAD + SPAN]
            dx = along(center, 0)
            dy = along(window, 1)[:, PAD : PAD + SPAN]
            speeds = []
            for component in range(2):
                tiles = []
                for tile in range(4):
                    bc = lambda j: jnp.broadcast_to(
                        fine_y[plane, component, 8 * m + j : 8 * m + j + 1, :], (8, SPAN)
                    )
                    tiles.append(
                        share_a * bc(max(2 * tile - 1, 0))
                        + share_b * bc(2 * tile)
                        + share_c * bc(2 * tile + 1)
                    )
                flow[component, :, lanes] = jnp.concatenate(tiles[1:3], 0)
                speeds.append(jnp.concatenate(tiles, 0))
            value = center - (speeds[0] * dx + speeds[1] * dy)
            first[:, PAD + SPAN * m : PAD + SPAN * m + SPAN] = value
            if m == 0:
                first[:, PAD + NF :] = value[:, :PAD]
            if m == 3:
                first[:, 0:PAD] = value[:, SPAN - PAD :]
        for m in range(4):
            lanes = slice(SPAN * m, SPAN * m + SPAN)
            window = first[:, SPAN * m : SPAN * m + SPAN + 2 * PAD]
            center = window[:, PAD : PAD + SPAN]
            dx = along(center, 0)[8:24]
            dy = along(window[8:24], 1)[:, PAD : PAD + SPAN]
            out[plane, :, lanes] = 0.5 * (
                (scalar[plane, :, lanes] + center[8:24])
                - (flow[0, :, lanes] * dx + flow[1, :, lanes] * dy)
            )
        return carry

    lax.fori_loop(0, 4, plane_step, 0)


def spread_table():
    fine = np.arange(512)
    table = np.zeros((256, 512), np.float32)
    table[fine // 4, fine] += 1.0 - (fine % 4) / 4.0
    table[fine // 4 + 1, fine] += (fine % 4) / 4.0
    return table


def vmem():
    return pl.BlockSpec(memory_space=pltpu.VMEM)


def body(velocity_coef, scalar_field, plane_offset):
    table, send, turn, weight = tables()
    dma = pltpu.SemaphoreType.DMA
    blocks = (OUTER, INNER)
    next_coef, velocity, above, low, high = pl.pallas_call(
        spectral_kernel,
        out_shape=(
            jax.ShapeDtypeStruct(velocity_coef.shape, F32),
            jax.ShapeDtypeStruct((2, 8, NV), F32),
            jax.ShapeDtypeStruct((2, 8, NV), F32),
            jax.ShapeDtypeStruct((4, 8, NF), F32),
            jax.ShapeDtypeStruct((4, 8, NF), F32),
        ),
        in_specs=[vmem()] * 6,
        out_specs=tuple([vmem()] * 5),
        scratch_shapes=[
            pltpu.VMEM((2, 256, 128), F32),
            pltpu.VMEM(blocks + (2, 128), F32),
            pltpu.VMEM(blocks + (2, 128), F32),
            pltpu.VMEM(blocks + (2, 128), F32),
            pltpu.VMEM((2, 128, 128), F32),
            pltpu.VMEM(blocks + (1, 128), F32),
            pltpu.VMEM(blocks + (1, 128), F32),
            pltpu.VMEM(blocks + (1, 128), F32),
            dma((6,)),
            dma((6,)),
            dma((4, 4)),
            dma((2,)),
        ],
        compiler_params=pltpu.CompilerParams(collective_id=0, has_side_effects=True),
        name="spectral",
    )(velocity_coef, scalar_field, jnp.asarray(table), jnp.asarray(send), jnp.asarray(turn), jnp.asarray(weight))
    scalar_next = pl.pallas_call(
        transport_kernel,
        out_shape=jax.ShapeDtypeStruct(scalar_field.shape, F32),
        in_specs=[pl.BlockSpec(memory_space=pltpu.SMEM)] + [vmem()] * 6,
        out_specs=vmem(),
        scratch_shapes=[
            pltpu.VMEM((4, 32, NF + 2 * PAD), F32),
            pltpu.VMEM((32, NF + 2 * PAD), F32),
            pltpu.VMEM((4, 2, 32, 512), F32),
            pltpu.VMEM((2, 16, NF), F32),
        ],
        name="transport",
    )(plane_offset, scalar_field, low, high, velocity, above, jnp.asarray(spread_table(), jnp.bfloat16))
    return next_coef, scalar_next


def solution(mesh):
    in_specs = (P(None, None, "grp", "blk", None), P("grp", "blk", None), P("grp"))
    out_specs = (P(None, None, "grp", "blk", None), P("grp", "blk", None))
    return jax.shard_map(body, mesh=mesh, in_specs=in_specs, out_specs=out_specs, check_vma=False)
```

```python
import functools

import jax
import jax.numpy as jnp
import numpy as np
from jax import lax
from jax.experimental import pallas as pl
from jax.experimental.pallas import tpu as pltpu
from jax.sharding import PartitionSpec as P

TIME_STEP = 0.05
VISCOSITY = 0.5
STENCIL = (0.8, -0.2, 4.0 / 105.0, -1.0 / 280.0)
HIGHEST = lax.Precision.HIGHEST
MESH = pl.DeviceIdType.MESH
NV = 512
OUTER = 8
INNER = 16
BLOCKS = OUTER * INNER
F32 = jnp.float32
PAD = 128
NF = 2048
SPAN = 512


def tables():
    base = np.arange(128)
    angle = 2.0 * np.pi * ((base[:, None] * base[None, :]) % 128) / 128.0
    table = np.concatenate([np.cos(angle), np.sin(angle)], 1)
    wave = np.arange(NV)
    signed = np.where(2 * wave < NV, wave, wave - NV)
    wavenum = 2.0 * np.pi * signed / NV
    rows = np.arange(8) - 1
    ang_x = 2.0 * np.pi * ((rows[:, None] * wave[None, :]) % NV) / NV
    cos_x, sin_x = np.cos(ang_x) / NV, np.sin(ang_x) / NV
    send = np.stack([cos_x, sin_x, -wavenum * sin_x, wavenum * cos_x], 0)
    digit = np.arange(4)
    ang_d = 2.0 * np.pi * ((digit[:, None] * wave[None, :]) % NV) / NV
    turn = np.stack([np.cos(ang_d), np.sin(ang_d)], 0)
    lane_digit = (np.arange(128) // 16) % 4
    ky = 4 * base[:, None] + lane_digit[None, :]
    weight = wavenum[ky]
    as32 = lambda a: np.asarray(a, np.float32)
    return as32(table), as32(send), as32(turn), as32(weight)


def exchange(sent, passed, landed, sems, blk, grp):
    outer, inner = blk // INNER, blk % INNER

    own = pltpu.make_async_copy(sent.at[outer], passed.at[outer], sems.at[0])
    own.start()

    def first(k, carry):
        there = lax.rem(outer + k, OUTER)
        pltpu.make_async_remote_copy(
            sent.at[there], passed.at[outer], sems.at[1], sems.at[2],
            device_id=(grp, there * INNER + inner), device_id_type=MESH,
        ).start()
        return carry

    lax.fori_loop(1, OUTER, first, 0)

    def rest():
        some = pl.ds(0, OUTER - 1)
        every = pltpu.make_async_remote_copy(
            sent.at[some], passed.at[some], sems.at[1], sems.at[2],
            device_id=(grp, lax.rem(outer + 1, OUTER) * INNER + inner), device_id_type=MESH,
        )
        own.wait()
        every.wait_recv()
        mine = pltpu.make_async_copy(passed.at[:, inner], landed.at[:, inner], sems.at[3])
        mine.start()

        def second(k, carry):
            there = lax.rem(inner + k, INNER)
            pltpu.make_async_remote_copy(
                passed.at[:, there], landed.at[:, inner], sems.at[4], sems.at[5],
                device_id=(grp, outer * INNER + there), device_id_type=MESH,
            ).start()
            return carry

        lax.fori_loop(1, INNER, second, 0)
        every.wait_send()

        def finish():
            part = pl.ds(0, INNER - 1)
            whole = pltpu.make_async_remote_copy(
                passed.at[:, part], landed.at[:, part], sems.at[4], sems.at[5],
                device_id=(grp, outer * INNER + lax.rem(inner + 1, INNER)), device_id_type=MESH,
            )
            mine.wait()
            whole.wait_recv()
            whole.wait_send()

        return finish

    return rest


def step_kernel(
    offset, coef, scalar, table, send, turn, weight, spread,
    next_coef, out,
    pack, sent, passed, landed, pack2, sent2, passed2, landed2,
    velocity, above, field, slope, first, fine_y, flow,
    sems, sems2, halo_sems, grp_sems, own_sem,
):
    blk = lax.axis_index("blk")
    grp = lax.axis_index("grp")
    outer, inner = blk // INNER, blk % INNER
    behind, ahead = lax.rem(blk + BLOCKS - 1, BLOCKS), lax.rem(blk + 1, BLOCKS)
    groups = lax.axis_size("grp")
    below, upper = lax.rem(grp + groups - 1, groups), lax.rem(grp + 1, groups)

    barrier = pltpu.get_barrier_semaphore()

    def hello(device):
        pl.semaphore_signal(barrier, inc=1, device_id=device, device_id_type=MESH)

    def greet_outer(k, carry):
        hello((grp, lax.rem(outer + k, OUTER) * INNER + inner))
        return carry

    def greet_inner(k, carry):
        hello((grp, outer * INNER + lax.rem(inner + k, INNER)))
        return carry

    hello((grp, behind))
    hello((grp, ahead))
    hello((upper, blk))
    lax.fori_loop(1, OUTER, greet_outer, 0)
    lax.fori_loop(1, INNER, greet_inner, 0)
    whole = pl.ds(PAD, NF)
    own = [
        pltpu.make_async_copy(
            scalar.at[plane], field.at[plane, pl.ds(8, 16), whole], own_sem.at[plane]
        )
        for plane in range(4)
    ]
    for copy in own:
        copy.start()

    real = jnp.concatenate([coef[0, 0, 0], coef[1, 0, 0]], 0)
    imag = jnp.concatenate([coef[0, 1, 0], coef[1, 1, 0]], 0)
    for row in range(8):
        for kind in range(2):
            re, im = 0.0, 0.0
            for digit in range(4):
                lanes = slice(128 * digit, 128 * digit + 128)
                tr = send[2 * kind, row : row + 1, lanes]
                ti = send[2 * kind + 1, row : row + 1, lanes]
                re = re + (tr * real[:, lanes] - ti * imag[:, lanes])
                im = im + (tr * imag[:, lanes] + ti * real[:, lanes])
            start = 128 * kind + row
            pack[0, pl.ds(start, 8, 16), :] = re
            pack[1, pl.ds(start, 8, 16), :] = -im
            pack[0, pl.ds(start + 8, 8, 16), :] = im
            pack[1, pl.ds(start + 8, 8, 16), :] = re
    along_x = lax.dot_general(
        table[...], jnp.concatenate([pack[0], pack[1]], 1), (((1,), (1,)), ((), ())), precision=HIGHEST,
        preferred_element_type=F32,
    )
    for part in range(OUTER):
        rows = slice(part * INNER, part * INNER + INNER)
        sent[part, :, 0, :] = along_x[rows, 0:128]
        sent[part, :, 1, :] = along_x[rows, 128:256]

    pl.semaphore_wait(barrier, OUTER - 1 + INNER - 1 + 3)

    step = exchange(sent, passed, landed, sems, blk, grp)
    halos = []
    for plane in range(4):
        halos.append(pltpu.make_async_remote_copy(
            scalar.at[plane, pl.ds(8, 8)], field.at[plane, pl.ds(0, 8), whole],
            halo_sems.at[0, plane], halo_sems.at[1, plane],
            device_id=(grp, ahead), device_id_type=MESH,
        ))
        halos.append(pltpu.make_async_remote_copy(
            scalar.at[plane, pl.ds(0, 8)], field.at[plane, pl.ds(24, 8), whole],
            halo_sems.at[2, plane], halo_sems.at[3, plane],
            device_id=(grp, behind), device_id_type=MESH,
        ))
    for copy in halos:
        copy.start()
    step()()

    vel_in = jnp.concatenate([landed[part, :, 0, :] for part in range(OUTER)], 0)
    der_in = jnp.concatenate([landed[part, :, 1, :] for part in range(OUTER)], 0)
    stacked = jnp.concatenate([vel_in.T, (vel_in * weight[...]).T, der_in.T], 0)
    along_y = jnp.dot(stacked, table[...], precision=HIGHEST, preferred_element_type=F32)

    def synthesize(kind, component):
        parts = [0.0] * 4
        for digit in range(4):
            start = 128 * kind + (component * 4 + digit) * 16
            cos_re = along_y[start : start + 8, 0:128]
            sin_re = along_y[start : start + 8, 128:256]
            cos_im = along_y[start + 8 : start + 16, 0:128]
            sin_im = along_y[start + 8 : start + 16, 128:256]
            if kind == 1:
                head_re, head_im = -cos_im - sin_re, cos_re - sin_im
            else:
                head_re, head_im = cos_re - sin_im, sin_re + cos_im
            for part in range(4):
                lanes = slice(128 * part, 128 * part + 128)
                tr = turn[0, digit : digit + 1, lanes]
                ti = turn[1, digit : digit + 1, lanes]
                parts[part] = parts[part] + (tr * head_re - ti * head_im)
        return parts

    vel = [synthesize(0, 0), synthesize(0, 1)]
    for component in range(2):
        for part in range(4):
            velocity[component, :, 128 * part : 128 * part + 128] = vel[component][part]
    lift = pltpu.make_async_remote_copy(
        velocity, above, grp_sems.at[0], grp_sems.at[1],
        device_id=(below, blk), device_id_type=MESH,
    )
    lift.start()

    for component in range(2):
        grad_y = synthesize(1, component)
        grad_x = synthesize(2, component)
        adv = [vel[0][a] * grad_x[a] + vel[1][a] * grad_y[a] for a in range(4)]
        even, odd = adv[0] + adv[2], adv[1] + adv[3]
        even_d, odd_d = adv[0] - adv[2], adv[1] - adv[3]
        heads = [(even + odd, None), (even_d, -odd_d), (even - odd, None), (even_d, odd_d)]
        for digit, (p, q) in enumerate(heads):
            tr = turn[0, digit : digit + 1, 0:128]
            ti = turn[1, digit : digit + 1, 0:128]
            if q is None:
                re, im = p * tr, -(p * ti)
            else:
                re, im = p * tr + q * ti, q * tr - p * ti
            start = component * 4 + digit
            pack2[0, pl.ds(start, 8, 16), :] = re
            pack2[1, pl.ds(start, 8, 16), :] = im
            pack2[0, pl.ds(start + 8, 8, 16), :] = im
            pack2[1, pl.ds(start + 8, 8, 16), :] = -re
    forward_y = lax.dot_general(
        table[...], jnp.concatenate([pack2[0], pack2[1]], 1), (((1,), (1,)), ((), ())), precision=HIGHEST,
        preferred_element_type=F32,
    )
    for part in range(OUTER):
        sent2[part, :, 0, :] = forward_y[part * INNER : part * INNER + INNER]
    step = exchange(sent2, passed2, landed2, sems2, blk, grp)
    for copy in own + halos:
        copy.wait()
    lax.fori_loop(0, 4, functools.partial(slopes, field, slope), 0)
    finish = step()
    lift.wait()
    refine_along_y(offset, velocity, above, spread, fine_y)
    lax.fori_loop(0, 4, functools.partial(sections, field, slope, first, fine_y, flow, out), 0)
    finish()

    back = jnp.concatenate([landed2[part, :, 0, :] for part in range(OUTER)], 0)
    along = jnp.dot(back.T, table[...], precision=HIGHEST, preferred_element_type=F32)
    heads = []
    for row in range(1, 5):
        start = row * 16
        cos_re = along[start : start + 8, 0:128]
        sin_re = along[start : start + 8, 128:256]
        cos_im = along[start + 8 : start + 16, 0:128]
        sin_im = along[start + 8 : start + 16, 128:256]
        heads.append((cos_re + sin_im, cos_im - sin_re))
    row_index = lax.broadcasted_iota(jnp.int32, (8, 128), 0) % 4 + blk * 4
    row_signed = jnp.where(2 * row_index < NV, row_index, row_index - NV)
    row_wave = row_signed.astype(F32) * (2.0 * np.pi / NV)
    lane = lax.broadcasted_iota(jnp.int32, (8, 128), 1)
    for part in range(4):
        lanes = slice(128 * part, 128 * part + 128)
        re, im = 0.0, 0.0
        for digit, (head_re, head_im) in enumerate(heads):
            tr = turn[0, digit : digit + 1, lanes]
            ti = turn[1, digit : digit + 1, lanes]
            re = re + (tr * head_re + ti * head_im)
            im = im + (tr * head_im - ti * head_re)
        column = lane + 128 * part
        column_signed = column if part < 2 else column - NV
        column_wave = column_signed.astype(F32) * (2.0 * np.pi / NV)
        keep = (3 * jnp.abs(row_signed) < NV) & (3 * jnp.abs(column_signed) < NV)
        gain = jnp.where(keep, TIME_STEP / NV, 0.0)
        damping = jnp.exp(-VISCOSITY * TIME_STEP * (row_wave * row_wave + column_wave * column_wave))
        new_re = damping * (real[:, lanes] - gain * re)
        new_im = damping * (imag[:, lanes] - gain * im)
        for component in range(2):
            rows = slice(4 * component, 4 * component + 4)
            next_coef[component, 0, 0, :, lanes] = new_re[rows]
            next_coef[component, 1, 0, :, lanes] = new_im[rows]

def refine_along_y(offset, velocity, above, spread, fine_y):
    for plane in range(4):
        fraction = (offset[plane] % 16).astype(F32) * 0.0625
        for component in range(2):
            mixed = (1.0 - fraction) * velocity[component] + fraction * above[component]
            wide = jnp.concatenate([mixed, mixed[:, :128]], 1)
            rows = jnp.concatenate([wide[:, 128 * m : 128 * m + 256] for m in range(4)], 0)
            top = rows.astype(jnp.bfloat16)
            rest = (rows - top.astype(F32)).astype(jnp.bfloat16)
            fine_y[plane, component] = jnp.dot(
                top, spread[...], preferred_element_type=F32
            ) + jnp.dot(rest, spread[...], preferred_element_type=F32)


def along(values, axis):
    size = values.shape[axis]
    total = 0.0
    for shift, weight in zip((1, 2, 3, 4), STENCIL):
        total = total + (TIME_STEP * 4.0 * weight) * (
            pltpu.roll(values, size - shift, axis) - pltpu.roll(values, shift, axis)
        )
    return total


def slopes(field, slope, plane, carry):
    field[plane, :, 0:PAD] = field[plane, :, NF : NF + PAD]
    field[plane, :, PAD + NF : NF + 2 * PAD] = field[plane, :, PAD : 2 * PAD]
    for m in range(4):
        lanes = slice(SPAN * m, SPAN * m + SPAN)
        window = field[plane, :, SPAN * m : SPAN * m + SPAN + 2 * PAD]
        slope[plane, 0, :, lanes] = along(window[:, PAD : PAD + SPAN], 0)
        slope[plane, 1, :, lanes] = along(window, 1)[:, PAD : PAD + SPAN]
    return carry


def sections(field, slope, first, fine_y, flow, out, plane, carry):
    index = lax.broadcasted_iota(jnp.int32, (8, SPAN), 0)
    share = (index % 4).astype(F32) * 0.25
    half = index < 4
    share_a = jnp.where(half, 1.0 - share, 0.0)
    share_b = jnp.where(half, share, 1.0 - share)
    share_c = jnp.where(half, 0.0, share)
    for m in range(4):
        lanes = slice(SPAN * m, SPAN * m + SPAN)
        inside = slice(PAD + SPAN * m, PAD + SPAN * m + SPAN)
        for tile in range(4):
            rows = slice(8 * tile, 8 * tile + 8)
            speeds = []
            for component in range(2):
                bc = lambda j: jnp.broadcast_to(
                    fine_y[plane, component, 8 * m + j : 8 * m + j + 1, :], (8, SPAN)
                )
                speeds.append(
                    share_a * bc(max(2 * tile - 1, 0))
                    + share_b * bc(2 * tile)
                    + share_c * bc(2 * tile + 1)
                )
                if tile in (1, 2):
                    flow[component, 8 * tile - 8 : 8 * tile, lanes] = speeds[component]
            value = field[plane, rows, inside] - (
                speeds[0] * slope[plane, 0, rows, lanes] + speeds[1] * slope[plane, 1, rows, lanes]
            )
            first[rows, inside] = value
            if m == 0:
                first[rows, PAD + NF : NF + 2 * PAD] = value[:, :PAD]
            if m == 3:
                first[rows, 0:PAD] = value[:, SPAN - PAD :]
    for m in range(4):
        lanes = slice(SPAN * m, SPAN * m + SPAN)
        window = first[:, SPAN * m : SPAN * m + SPAN + 2 * PAD]
        center = window[:, PAD : PAD + SPAN]
        dx = along(center, 0)[8:24]
        dy = along(window[8:24], 1)[:, PAD : PAD + SPAN]
        out[plane, :, lanes] = 0.5 * (
            (field[plane, 8:24, PAD + SPAN * m : PAD + SPAN * m + SPAN] + center[8:24])
            - (flow[0, :, lanes] * dx + flow[1, :, lanes] * dy)
        )
    return carry


def spread_table():
    fine = np.arange(512)
    table = np.zeros((256, 512), np.float32)
    table[fine // 4, fine] += 1.0 - (fine % 4) / 4.0
    table[fine // 4 + 1, fine] += (fine % 4) / 4.0
    return table


def vmem():
    return pl.BlockSpec(memory_space=pltpu.VMEM)


def body(velocity_coef, scalar_field, plane_offset):
    table, send, turn, weight = tables()
    dma = pltpu.SemaphoreType.DMA
    blocks = (OUTER, INNER)
    return pl.pallas_call(
        step_kernel,
        out_shape=(
            jax.ShapeDtypeStruct(velocity_coef.shape, F32),
            jax.ShapeDtypeStruct(scalar_field.shape, F32),
        ),
        in_specs=[
            pl.BlockSpec(memory_space=pltpu.SMEM), vmem(), pl.BlockSpec(memory_space=pl.ANY),
            vmem(), vmem(), vmem(), vmem(), vmem(),
        ],
        out_specs=(vmem(), vmem()),
        scratch_shapes=[
            pltpu.VMEM((2, 256, 128), F32),
            pltpu.VMEM(blocks + (2, 128), F32),
            pltpu.VMEM(blocks + (2, 128), F32),
            pltpu.VMEM(blocks + (2, 128), F32),
            pltpu.VMEM((2, 128, 128), F32),
            pltpu.VMEM(blocks + (1, 128), F32),
            pltpu.VMEM(blocks + (1, 128), F32),
            pltpu.VMEM(blocks + (1, 128), F32),
            pltpu.VMEM((2, 8, NV), F32),
            pltpu.VMEM((2, 8, NV), F32),
            pltpu.VMEM((4, 32, NF + 2 * PAD), F32),
            pltpu.VMEM((4, 2, 32, NF), F32),
            pltpu.VMEM((32, NF + 2 * PAD), F32),
            pltpu.VMEM((4, 2, 32, SPAN), F32),
            pltpu.VMEM((2, 16, NF), F32),
            dma((6,)),
            dma((6,)),
            dma((4, 4)),
            dma((2,)),
            dma((4,)),
        ],
        compiler_params=pltpu.CompilerParams(collective_id=0, has_side_effects=True),
        name="step",
    )(
        plane_offset, velocity_coef, scalar_field, jnp.asarray(table), jnp.asarray(send),
        jnp.asarray(turn), jnp.asarray(weight), jnp.asarray(spread_table(), jnp.bfloat16),
    )


def solution(mesh):
    in_specs = (P(None, None, "grp", "blk", None), P("grp", "blk", None), P("grp"))
    out_specs = (P(None, None, "grp", "blk", None), P("grp", "blk", None))
    return jax.shard_map(body, mesh=mesh, in_specs=in_specs, out_specs=out_specs, check_vma=False)
```

```python
import functools

import jax
import jax.numpy as jnp
import numpy as np
from jax import lax
from jax.experimental import pallas as pl
from jax.experimental.pallas import tpu as pltpu
from jax.sharding import PartitionSpec as P

TIME_STEP = 0.05
VISCOSITY = 0.5
STENCIL = (0.8, -0.2, 4.0 / 105.0, -1.0 / 280.0)
PRECISE = lax.Precision.HIGH
MESH = pl.DeviceIdType.MESH
NV = 512
OUTER = 8
INNER = 16
COLUMNS, HALVES = 4, 2
BLOCKS = OUTER * INNER
F32 = jnp.float32
PAD = 128
NF = 2048
SPAN = 512


def tables():
    base = np.arange(128)
    angle = 2.0 * np.pi * ((base[:, None] * base[None, :]) % 128) / 128.0
    table = np.concatenate([np.cos(angle), np.sin(angle)], 1)
    wave = np.arange(NV)
    signed = np.where(2 * wave < NV, wave, wave - NV)
    wavenum = 2.0 * np.pi * signed / NV
    rows = np.arange(8) - 1
    ang_x = 2.0 * np.pi * ((rows[:, None] * wave[None, :]) % NV) / NV
    cos_x, sin_x = np.cos(ang_x) / NV, np.sin(ang_x) / NV
    send = np.stack([cos_x, sin_x, -wavenum * sin_x, wavenum * cos_x], 0)
    digit = np.arange(4)
    ang_d = 2.0 * np.pi * ((digit[:, None] * wave[None, :]) % NV) / NV
    turn = np.stack([np.cos(ang_d), np.sin(ang_d)], 0)
    lane_digit = (np.arange(128) // 16) % 4
    ky = 4 * base[:, None] + lane_digit[None, :]
    weight = wavenum[ky]
    as32 = lambda a: np.asarray(a, np.float32)
    return as32(table), as32(send), as32(turn), as32(weight)


def exchange(sent, passed, landed, sems, blk, grp):
    outer, inner = blk // INNER, blk % INNER
    column, half = outer // HALVES, outer % HALVES
    other = 1 - half

    def to_column(there, side, group):
        return pltpu.make_async_remote_copy(
            sent.at[there, side], passed.at[half, column], sems.at[0, group], sems.at[1, group],
            device_id=(grp, (there * HALVES + side) * INNER + inner), device_id_type=MESH,
        )

    def far(k, carry):
        to_column(lax.rem(column + k, COLUMNS), other, 0).start()
        return carry

    def near(k, carry):
        to_column(lax.rem(column + k, COLUMNS), half, 1).start()
        return carry

    lax.fori_loop(0, COLUMNS, far, 0)
    own = pltpu.make_async_copy(sent.at[column, half], passed.at[half, column], sems.at[2, 0])
    own.start()
    lax.fori_loop(1, COLUMNS, near, 0)

    def arrived(count, group):
        some = pl.ds(0, count)
        return pltpu.make_async_remote_copy(
            passed.at[0, some], passed.at[0, some], sems.at[0, group], sems.at[1, group],
            device_id=(grp, (lax.rem(column + 1, COLUMNS) * HALVES + half) * INNER + inner),
            device_id_type=MESH,
        )

    def spread_inner(side, group):
        mine = pltpu.make_async_copy(
            passed.at[side, :, inner], landed.at[side, :, inner], sems.at[2, group]
        )

        def one(k, carry):
            there = lax.rem(inner + k, INNER)
            pltpu.make_async_remote_copy(
                passed.at[side, :, there], landed.at[side, :, inner],
                sems.at[0, group], sems.at[1, group],
                device_id=(grp, outer * INNER + there), device_id_type=MESH,
            ).start()
            return carry

        lax.fori_loop(1, INNER, one, 0)
        mine.start()
        return mine

    def landed_whole(side, group):
        part = pl.ds(0, INNER - 1)
        return pltpu.make_async_remote_copy(
            passed.at[side, :, part], landed.at[side, :, part], sems.at[0, group], sems.at[1, group],
            device_id=(grp, outer * INNER + lax.rem(inner + 1, INNER)), device_id_type=MESH,
        )

    def pass_near():
        own.wait()
        arrived(COLUMNS - 1, 1).wait_recv()
        mine_near = spread_inner(half, 2)

        def pass_far():
            arrived(COLUMNS, 0).wait_recv()
            mine_far = spread_inner(other, 3)

            def finish():
                mine_near.wait()
                mine_far.wait()
                landed_whole(half, 2).wait_recv()
                landed_whole(other, 3).wait_recv()

            def drain():
                arrived(COLUMNS - 1, 1).wait_send()
                arrived(COLUMNS, 0).wait_send()
                landed_whole(half, 2).wait_send()
                landed_whole(other, 3).wait_send()

            return finish, drain

        return pass_far

    return pass_near


def step_kernel(
    offset, coef, scalar, table, send, turn, weight, spread,
    next_coef, out,
    pack, sent, passed, landed, pack2, sent2, passed2, landed2,
    velocity, above, field, slope, first, fine_y, flow,
    sems, sems2, halo_sems, grp_sems, own_sem,
):
    blk = lax.axis_index("blk")
    grp = lax.axis_index("grp")
    outer, inner = blk // INNER, blk % INNER
    behind, ahead = lax.rem(blk + BLOCKS - 1, BLOCKS), lax.rem(blk + 1, BLOCKS)
    groups = lax.axis_size("grp")
    below, upper = lax.rem(grp + groups - 1, groups), lax.rem(grp + 1, groups)

    barrier = pltpu.get_barrier_semaphore()

    def hello(device):
        pl.semaphore_signal(barrier, inc=1, device_id=device, device_id_type=MESH)

    def greet_outer(k, carry):
        hello((grp, lax.rem(outer + k, OUTER) * INNER + inner))
        return carry

    def greet_inner(k, carry):
        hello((grp, outer * INNER + lax.rem(inner + k, INNER)))
        return carry

    hello((grp, behind))
    hello((grp, ahead))
    hello((upper, blk))
    lax.fori_loop(1, OUTER, greet_outer, 0)
    lax.fori_loop(1, INNER, greet_inner, 0)
    whole = pl.ds(PAD, NF)
    own = [
        pltpu.make_async_copy(
            scalar.at[plane], field.at[plane, pl.ds(8, 16), whole], own_sem.at[plane]
        )
        for plane in range(4)
    ]
    for copy in own:
        copy.start()

    real = jnp.concatenate([coef[0, 0, 0], coef[1, 0, 0]], 0)
    imag = jnp.concatenate([coef[0, 1, 0], coef[1, 1, 0]], 0)
    for row in range(8):
        for kind in range(2):
            re, im = 0.0, 0.0
            for digit in range(4):
                lanes = slice(128 * digit, 128 * digit + 128)
                tr = send[2 * kind, row : row + 1, lanes]
                ti = send[2 * kind + 1, row : row + 1, lanes]
                re = re + (tr * real[:, lanes] - ti * imag[:, lanes])
                im = im + (tr * imag[:, lanes] + ti * real[:, lanes])
            start = 128 * kind + row
            pack[0, pl.ds(start, 8, 16), :] = re
            pack[1, pl.ds(start, 8, 16), :] = -im
            pack[0, pl.ds(start + 8, 8, 16), :] = im
            pack[1, pl.ds(start + 8, 8, 16), :] = re
    along_x = lax.dot_general(
        table[...], jnp.concatenate([pack[0], pack[1]], 1), (((1,), (1,)), ((), ())), precision=PRECISE,
        preferred_element_type=F32,
    )
    for part in range(OUTER):
        rows = slice(part * INNER, part * INNER + INNER)
        sent[part // HALVES, part % HALVES, :, 0, :] = along_x[rows, 0:128]
        sent[part // HALVES, part % HALVES, :, 1, :] = along_x[rows, 128:256]

    pl.semaphore_wait(barrier, OUTER - 1 + INNER - 1 + 3)

    step = exchange(sent, passed, landed, sems, blk, grp)
    halos = []
    for plane in range(4):
        halos.append(pltpu.make_async_remote_copy(
            scalar.at[plane, pl.ds(8, 8)], field.at[plane, pl.ds(0, 8), whole],
            halo_sems.at[0, plane], halo_sems.at[1, plane],
            device_id=(grp, ahead), device_id_type=MESH,
        ))
        halos.append(pltpu.make_async_remote_copy(
            scalar.at[plane, pl.ds(0, 8)], field.at[plane, pl.ds(24, 8), whole],
            halo_sems.at[2, plane], halo_sems.at[3, plane],
            device_id=(grp, behind), device_id_type=MESH,
        ))
    for copy in halos:
        copy.start()
    finish, drain = step()()
    finish()

    vel_in = jnp.concatenate([landed[part % HALVES, part // HALVES, :, 0, :] for part in range(OUTER)], 0)
    der_in = jnp.concatenate([landed[part % HALVES, part // HALVES, :, 1, :] for part in range(OUTER)], 0)
    stacked = jnp.concatenate([vel_in.T, (vel_in * weight[...]).T, der_in.T], 0)
    along_y = jnp.dot(stacked, table[...], precision=PRECISE, preferred_element_type=F32)

    def synthesize(kind, component):
        parts = [0.0] * 4
        for digit in range(4):
            start = 128 * kind + (component * 4 + digit) * 16
            cos_re = along_y[start : start + 8, 0:128]
            sin_re = along_y[start : start + 8, 128:256]
            cos_im = along_y[start + 8 : start + 16, 0:128]
            sin_im = along_y[start + 8 : start + 16, 128:256]
            if kind == 1:
                head_re, head_im = -cos_im - sin_re, cos_re - sin_im
            else:
                head_re, head_im = cos_re - sin_im, sin_re + cos_im
            for part in range(4):
                lanes = slice(128 * part, 128 * part + 128)
                tr = turn[0, digit : digit + 1, lanes]
                ti = turn[1, digit : digit + 1, lanes]
                parts[part] = parts[part] + (tr * head_re - ti * head_im)
        return parts

    vel = [synthesize(0, 0), synthesize(0, 1)]
    for component in range(2):
        for part in range(4):
            velocity[component, :, 128 * part : 128 * part + 128] = vel[component][part]
    lift = pltpu.make_async_remote_copy(
        velocity, above, grp_sems.at[0], grp_sems.at[1],
        device_id=(below, blk), device_id_type=MESH,
    )
    lift.start()

    for component in range(2):
        grad_y = synthesize(1, component)
        grad_x = synthesize(2, component)
        adv = [vel[0][a] * grad_x[a] + vel[1][a] * grad_y[a] for a in range(4)]
        even, odd = adv[0] + adv[2], adv[1] + adv[3]
        even_d, odd_d = adv[0] - adv[2], adv[1] - adv[3]
        heads = [(even + odd, None), (even_d, -odd_d), (even - odd, None), (even_d, odd_d)]
        for digit, (p, q) in enumerate(heads):
            tr = turn[0, digit : digit + 1, 0:128]
            ti = turn[1, digit : digit + 1, 0:128]
            if q is None:
                re, im = p * tr, -(p * ti)
            else:
                re, im = p * tr + q * ti, q * tr - p * ti
            start = component * 4 + digit
            pack2[0, pl.ds(start, 8, 16), :] = re
            pack2[1, pl.ds(start, 8, 16), :] = im
            pack2[0, pl.ds(start + 8, 8, 16), :] = im
            pack2[1, pl.ds(start + 8, 8, 16), :] = -re
    forward_y = lax.dot_general(
        table[...], jnp.concatenate([pack2[0], pack2[1]], 1), (((1,), (1,)), ((), ())), precision=PRECISE,
        preferred_element_type=F32,
    )
    for part in range(OUTER):
        sent2[part // HALVES, part % HALVES, :, 0, :] = forward_y[part * INNER : part * INNER + INNER]
    step = exchange(sent2, passed2, landed2, sems2, blk, grp)
    for copy in own + halos:
        copy.wait()
    lax.fori_loop(0, 4, functools.partial(slopes, field, slope), 0)
    step = step()
    lift.wait_recv()
    refine_along_y(offset, velocity, above, spread, fine_y)
    transport = functools.partial(sections, field, slope, first, fine_y, flow, out)
    lax.fori_loop(0, 2, transport, 0)
    finish2, drain2 = step()
    lax.fori_loop(2, 4, transport, 0)
    finish2()

    back = jnp.concatenate([landed2[part % HALVES, part // HALVES, :, 0, :] for part in range(OUTER)], 0)
    along = jnp.dot(back.T, table[...], precision=PRECISE, preferred_element_type=F32)
    heads = []
    for row in range(1, 5):
        start = row * 16
        cos_re = along[start : start + 8, 0:128]
        sin_re = along[start : start + 8, 128:256]
        cos_im = along[start + 8 : start + 16, 0:128]
        sin_im = along[start + 8 : start + 16, 128:256]
        heads.append((cos_re + sin_im, cos_im - sin_re))
    row_index = lax.broadcasted_iota(jnp.int32, (8, 128), 0) % 4 + blk * 4
    row_signed = jnp.where(2 * row_index < NV, row_index, row_index - NV)
    row_wave = row_signed.astype(F32) * (2.0 * np.pi / NV)
    lane = lax.broadcasted_iota(jnp.int32, (8, 128), 1)
    for part in range(4):
        lanes = slice(128 * part, 128 * part + 128)
        re, im = 0.0, 0.0
        for digit, (head_re, head_im) in enumerate(heads):
            tr = turn[0, digit : digit + 1, lanes]
            ti = turn[1, digit : digit + 1, lanes]
            re = re + (tr * head_re + ti * head_im)
            im = im + (tr * head_im - ti * head_re)
        column = lane + 128 * part
        column_signed = column if part < 2 else column - NV
        column_wave = column_signed.astype(F32) * (2.0 * np.pi / NV)
        keep = (3 * jnp.abs(row_signed) < NV) & (3 * jnp.abs(column_signed) < NV)
        gain = jnp.where(keep, TIME_STEP / NV, 0.0)
        damping = jnp.exp(-VISCOSITY * TIME_STEP * (row_wave * row_wave + column_wave * column_wave))
        new_re = damping * (real[:, lanes] - gain * re)
        new_im = damping * (imag[:, lanes] - gain * im)
        for component in range(2):
            rows = slice(4 * component, 4 * component + 4)
            next_coef[component, 0, 0, :, lanes] = new_re[rows]
            next_coef[component, 1, 0, :, lanes] = new_im[rows]
    lift.wait_send()
    drain()
    drain2()

def refine_along_y(offset, velocity, above, spread, fine_y):
    for plane in range(4):
        fraction = (offset[plane] % 16).astype(F32) * 0.0625
        for component in range(2):
            mixed = (1.0 - fraction) * velocity[component] + fraction * above[component]
            wide = jnp.concatenate([mixed, mixed[:, :128]], 1)
            rows = jnp.concatenate([wide[:, 128 * m : 128 * m + 256] for m in range(4)], 0)
            top = rows.astype(jnp.bfloat16)
            rest = (rows - top.astype(F32)).astype(jnp.bfloat16)
            fine_y[plane, component] = jnp.dot(
                top, spread[...], preferred_element_type=F32
            ) + jnp.dot(rest, spread[...], preferred_element_type=F32)


def along(values, axis):
    size = values.shape[axis]
    total = 0.0
    for shift, weight in zip((1, 2, 3, 4), STENCIL):
        total = total + (TIME_STEP * 4.0 * weight) * (
            pltpu.roll(values, size - shift, axis) - pltpu.roll(values, shift, axis)
        )
    return total


def slopes(field, slope, plane, carry):
    field[plane, :, 0:PAD] = field[plane, :, NF : NF + PAD]
    field[plane, :, PAD + NF : NF + 2 * PAD] = field[plane, :, PAD : 2 * PAD]
    for m in range(4):
        lanes = slice(SPAN * m, SPAN * m + SPAN)
        window = field[plane, :, SPAN * m : SPAN * m + SPAN + 2 * PAD]
        slope[plane, 0, :, lanes] = along(window[:, PAD : PAD + SPAN], 0)
        slope[plane, 1, :, lanes] = along(window, 1)[:, PAD : PAD + SPAN]
    return carry


def sections(field, slope, first, fine_y, flow, out, plane, carry):
    index = lax.broadcasted_iota(jnp.int32, (8, SPAN), 0)
    share = (index % 4).astype(F32) * 0.25
    half = index < 4
    share_a = jnp.where(half, 1.0 - share, 0.0)
    share_b = jnp.where(half, share, 1.0 - share)
    share_c = jnp.where(half, 0.0, share)
    for m in range(4):
        lanes = slice(SPAN * m, SPAN * m + SPAN)
        inside = slice(PAD + SPAN * m, PAD + SPAN * m + SPAN)
        for tile in range(4):
            rows = slice(8 * tile, 8 * tile + 8)
            speeds = []
            for component in range(2):
                bc = lambda j: jnp.broadcast_to(
                    fine_y[plane, component, 8 * m + j : 8 * m + j + 1, :], (8, SPAN)
                )
                speeds.append(
                    share_a * bc(max(2 * tile - 1, 0))
                    + share_b * bc(2 * tile)
                    + share_c * bc(2 * tile + 1)
                )
                if tile in (1, 2):
                    flow[component, 8 * tile - 8 : 8 * tile, lanes] = speeds[component]
            value = field[plane, rows, inside] - (
                speeds[0] * slope[plane, 0, rows, lanes] + speeds[1] * slope[plane, 1, rows, lanes]
            )
            first[rows, inside] = value
            if m == 0:
                first[rows, PAD + NF : NF + 2 * PAD] = value[:, :PAD]
            if m == 3:
                first[rows, 0:PAD] = value[:, SPAN - PAD :]
    for m in range(4):
        lanes = slice(SPAN * m, SPAN * m + SPAN)
        window = first[:, SPAN * m : SPAN * m + SPAN + 2 * PAD]
        center = window[:, PAD : PAD + SPAN]
        dx = along(center, 0)[8:24]
        dy = along(window[8:24], 1)[:, PAD : PAD + SPAN]
        out[plane, :, lanes] = 0.5 * (
            (field[plane, 8:24, PAD + SPAN * m : PAD + SPAN * m + SPAN] + center[8:24])
            - (flow[0, :, lanes] * dx + flow[1, :, lanes] * dy)
        )
    return carry


def place_kernel(coef, scalar, coef_out, scalar_out, coef_buffer, scalar_buffer, sems):
    routes = [(coef, coef_buffer, coef_out)] + [
        (scalar.at[plane], scalar_buffer.at[plane], scalar_out.at[plane]) for plane in range(4)
    ]
    loads = [pltpu.make_async_copy(a, b, sems.at[0, k]) for k, (a, b, c) in enumerate(routes)]
    stores = [pltpu.make_async_copy(b, c, sems.at[1, k]) for k, (a, b, c) in enumerate(routes)]
    for copy in loads:
        copy.start()
    for load, store in zip(loads, stores):
        load.wait()
        store.start()
    for copy in stores:
        copy.wait()


def spread_table():
    fine = np.arange(512)
    table = np.zeros((256, 512), np.float32)
    table[fine // 4, fine] += 1.0 - (fine % 4) / 4.0
    table[fine // 4 + 1, fine] += (fine % 4) / 4.0
    return table


def vmem():
    return pl.BlockSpec(memory_space=pltpu.VMEM)


def body(velocity_coef, scalar_field, plane_offset):
    table, send, turn, weight = tables()
    dma = pltpu.SemaphoreType.DMA
    results = pl.pallas_call(
        step_kernel,
        out_shape=(
            jax.ShapeDtypeStruct(velocity_coef.shape, F32),
            jax.ShapeDtypeStruct(scalar_field.shape, F32),
        ),
        in_specs=[
            pl.BlockSpec(memory_space=pltpu.SMEM), vmem(), pl.BlockSpec(memory_space=pl.ANY),
            vmem(), vmem(), vmem(), vmem(), vmem(),
        ],
        out_specs=(vmem(), vmem()),
        scratch_shapes=[
            pltpu.VMEM((2, 256, 128), F32),
            pltpu.VMEM((COLUMNS, HALVES, INNER, 2, 128), F32),
            pltpu.VMEM((HALVES, COLUMNS, INNER, 2, 128), F32),
            pltpu.VMEM((HALVES, COLUMNS, INNER, 2, 128), F32),
            pltpu.VMEM((2, 128, 128), F32),
            pltpu.VMEM((COLUMNS, HALVES, INNER, 1, 128), F32),
            pltpu.VMEM((HALVES, COLUMNS, INNER, 1, 128), F32),
            pltpu.VMEM((HALVES, COLUMNS, INNER, 1, 128), F32),
            pltpu.VMEM((2, 8, NV), F32),
            pltpu.VMEM((2, 8, NV), F32),
            pltpu.VMEM((4, 32, NF + 2 * PAD), F32),
            pltpu.VMEM((4, 2, 32, NF), F32),
            pltpu.VMEM((32, NF + 2 * PAD), F32),
            pltpu.VMEM((4, 2, 32, SPAN), F32),
            pltpu.VMEM((2, 16, NF), F32),
            dma((3, 4)),
            dma((3, 4)),
            dma((4, 4)),
            dma((2,)),
            dma((4,)),
        ],
        compiler_params=pltpu.CompilerParams(collective_id=0, has_side_effects=True),
        name="step",
    )(
        plane_offset, velocity_coef, scalar_field, jnp.asarray(table), jnp.asarray(send),
        jnp.asarray(turn), jnp.asarray(weight), jnp.asarray(spread_table(), jnp.bfloat16),
    )
    anywhere = pl.BlockSpec(memory_space=pl.ANY)
    return pl.pallas_call(
        place_kernel,
        out_shape=(
            jax.ShapeDtypeStruct(velocity_coef.shape, F32),
            jax.ShapeDtypeStruct(scalar_field.shape, F32),
        ),
        in_specs=[anywhere, anywhere],
        out_specs=(anywhere, anywhere),
        scratch_shapes=[
            pltpu.VMEM(velocity_coef.shape, F32),
            pltpu.VMEM(scalar_field.shape, F32),
            dma((2, 5)),
        ],
        name="place",
    )(*results)


def solution(mesh):
    in_specs = (P(None, None, "grp", "blk", None), P("grp", "blk", None), P("grp"))
    out_specs = (P(None, None, "grp", "blk", None), P("grp", "blk", None))
    return jax.shard_map(body, mesh=mesh, in_specs=in_specs, out_specs=out_specs, check_vma=False)
```

```python
import functools

import jax
import jax.numpy as jnp
import numpy as np
from jax import lax
from jax.experimental import pallas as pl
from jax.experimental.pallas import tpu as pltpu
from jax.sharding import PartitionSpec as P

TIME_STEP = 0.05
VISCOSITY = 0.5
STENCIL = (0.8, -0.2, 4.0 / 105.0, -1.0 / 280.0)
PRECISE = lax.Precision.HIGH
MESH = pl.DeviceIdType.MESH
NV = 512
OUTER = 8
INNER = 16
COLUMNS, HALVES = 4, 2
BLOCKS = OUTER * INNER
F32 = jnp.float32
PAD = 128
NF = 2048
SPAN = 512


def tables():
    base = np.arange(128)
    angle = 2.0 * np.pi * ((base[:, None] * base[None, :]) % 128) / 128.0
    table = np.concatenate([np.cos(angle), np.sin(angle)], 1)
    wave = np.arange(NV)
    signed = np.where(2 * wave < NV, wave, wave - NV)
    wavenum = 2.0 * np.pi * signed / NV
    rows = np.arange(8) - 1
    ang_x = 2.0 * np.pi * ((rows[:, None] * wave[None, :]) % NV) / NV
    cos_x, sin_x = np.cos(ang_x) / NV, np.sin(ang_x) / NV
    send = np.stack([cos_x, sin_x, -wavenum * sin_x, wavenum * cos_x], 0)
    digit = np.arange(4)
    ang_d = 2.0 * np.pi * ((digit[:, None] * wave[None, :]) % NV) / NV
    turn = np.stack([np.cos(ang_d), np.sin(ang_d)], 0)
    lane_digit = (np.arange(128) // 16) % 4
    ky = 4 * base[:, None] + lane_digit[None, :]
    weight = wavenum[ky]
    as32 = lambda a: np.asarray(a, np.float32)
    return as32(table), as32(send), as32(turn), as32(weight)


def exchange(sent, passed, landed, sems, blk, grp):
    outer, inner = blk // INNER, blk % INNER
    column, half = outer // HALVES, outer % HALVES
    other = 1 - half

    def to_column(there, side, group):
        return pltpu.make_async_remote_copy(
            sent.at[there, side], passed.at[half, column], sems.at[0, group], sems.at[1, group],
            device_id=(grp, (there * HALVES + side) * INNER + inner), device_id_type=MESH,
        )

    def far(k, carry):
        to_column(lax.rem(column + 2 + k, COLUMNS), other, 0).start()
        return carry

    def near(k, carry):
        to_column(lax.rem(column + k, COLUMNS), half, 1).start()
        return carry

    lax.fori_loop(0, COLUMNS, far, 0)
    own = pltpu.make_async_copy(sent.at[column, half], passed.at[half, column], sems.at[2, 0])
    own.start()
    lax.fori_loop(1, COLUMNS, near, 0)

    def arrived(count, group):
        some = pl.ds(0, count)
        return pltpu.make_async_remote_copy(
            passed.at[0, some], passed.at[0, some], sems.at[0, group], sems.at[1, group],
            device_id=(grp, (lax.rem(column + 1, COLUMNS) * HALVES + half) * INNER + inner),
            device_id_type=MESH,
        )

    def spread_inner(side, group):
        mine = pltpu.make_async_copy(
            passed.at[side, :, inner], landed.at[side, :, inner], sems.at[2, group]
        )

        def one(k, carry):
            there = lax.rem(inner + k, INNER)
            pltpu.make_async_remote_copy(
                passed.at[side, :, there], landed.at[side, :, inner],
                sems.at[0, group], sems.at[1, group],
                device_id=(grp, outer * INNER + there), device_id_type=MESH,
            ).start()
            return carry

        lax.fori_loop(1, INNER, one, 0)
        mine.start()
        return mine

    def landed_whole(side, group):
        part = pl.ds(0, INNER - 1)
        return pltpu.make_async_remote_copy(
            passed.at[side, :, part], landed.at[side, :, part], sems.at[0, group], sems.at[1, group],
            device_id=(grp, outer * INNER + lax.rem(inner + 1, INNER)), device_id_type=MESH,
        )

    def pass_near():
        own.wait()
        arrived(COLUMNS - 1, 1).wait_recv()
        mine_near = spread_inner(half, 2)

        def pass_far():
            arrived(COLUMNS, 0).wait_recv()
            mine_far = spread_inner(other, 3)

            def finish():
                mine_near.wait()
                mine_far.wait()
                landed_whole(half, 2).wait_recv()
                landed_whole(other, 3).wait_recv()

            def drain():
                arrived(COLUMNS - 1, 1).wait_send()
                arrived(COLUMNS, 0).wait_send()
                landed_whole(half, 2).wait_send()
                landed_whole(other, 3).wait_send()

            return finish, drain

        return pass_far

    return pass_near


def step_kernel(
    offset, coef_in, scalar, table_in, send_in, turn_in, weight_in, spread_in,
    next_coef, out,
    pack, sent, passed, landed, pack2, sent2, passed2, landed2,
    velocity, above, field, slope, first, fine_y, flow,
    coef, table, send, turn, weight, spread, ready,
    sems, sems2, halo_sems, grp_sems, own_sem, load_sem, out_sem,
):
    blk = lax.axis_index("blk")
    grp = lax.axis_index("grp")
    outer, inner = blk // INNER, blk % INNER
    behind, ahead = lax.rem(blk + BLOCKS - 1, BLOCKS), lax.rem(blk + 1, BLOCKS)
    groups = lax.axis_size("grp")
    below, upper = lax.rem(grp + groups - 1, groups), lax.rem(grp + 1, groups)

    loads = [
        pltpu.make_async_copy(source, target, load_sem.at[k])
        for k, (source, target) in enumerate((
            (coef_in, coef), (send_in, send), (table_in, table),
            (weight_in, weight), (turn_in, turn), (spread_in, spread),
        ))
    ]
    for copy in loads:
        copy.start()

    barrier = pltpu.get_barrier_semaphore()

    def hello(device):
        pl.semaphore_signal(barrier, inc=1, device_id=device, device_id_type=MESH)

    column, side = outer // HALVES, outer % HALVES

    def greet_far(k, carry):
        hello((grp, (lax.rem(column + 2 + k, COLUMNS) * HALVES + 1 - side) * INNER + inner))
        return carry

    def greet_near(k, carry):
        hello((grp, (lax.rem(column + k, COLUMNS) * HALVES + side) * INNER + inner))
        return carry

    def greet_inner(k, carry):
        hello((grp, outer * INNER + lax.rem(inner + k, INNER)))
        return carry

    lax.fori_loop(0, COLUMNS, greet_far, 0)
    hello((grp, behind))
    hello((grp, ahead))
    hello((upper, blk))
    lax.fori_loop(1, COLUMNS, greet_near, 0)
    lax.fori_loop(1, INNER, greet_inner, 0)
    whole = pl.ds(PAD, NF)
    own = [
        pltpu.make_async_copy(
            scalar.at[plane], field.at[plane, pl.ds(8, 16), whole], own_sem.at[plane]
        )
        for plane in range(4)
    ]
    for copy in own:
        copy.start()

    for copy in loads:
        copy.wait()

    real = jnp.concatenate([coef[0, 0, 0], coef[1, 0, 0]], 0)
    imag = jnp.concatenate([coef[0, 1, 0], coef[1, 1, 0]], 0)
    for row in range(8):
        for kind in range(2):
            re, im = 0.0, 0.0
            for digit in range(4):
                lanes = slice(128 * digit, 128 * digit + 128)
                tr = send[2 * kind, row : row + 1, lanes]
                ti = send[2 * kind + 1, row : row + 1, lanes]
                re = re + (tr * real[:, lanes] - ti * imag[:, lanes])
                im = im + (tr * imag[:, lanes] + ti * real[:, lanes])
            start = 128 * kind + row
            pack[0, pl.ds(start, 8, 16), :] = re
            pack[1, pl.ds(start, 8, 16), :] = -im
            pack[0, pl.ds(start + 8, 8, 16), :] = im
            pack[1, pl.ds(start + 8, 8, 16), :] = re
    along_x = lax.dot_general(
        table[...], jnp.concatenate([pack[0], pack[1]], 1), (((1,), (1,)), ((), ())), precision=PRECISE,
        preferred_element_type=F32,
    )
    for part in range(OUTER):
        rows = slice(part * INNER, part * INNER + INNER)
        sent[part // HALVES, part % HALVES, :, 0, :] = along_x[rows, 0:128]
        sent[part // HALVES, part % HALVES, :, 1, :] = along_x[rows, 128:256]

    pl.semaphore_wait(barrier, OUTER - 1 + INNER - 1 + 3)

    step = exchange(sent, passed, landed, sems, blk, grp)
    halos = []
    for plane in range(4):
        halos.append(pltpu.make_async_remote_copy(
            scalar.at[plane, pl.ds(8, 8)], field.at[plane, pl.ds(0, 8), whole],
            halo_sems.at[0, plane], halo_sems.at[1, plane],
            device_id=(grp, ahead), device_id_type=MESH,
        ))
        halos.append(pltpu.make_async_remote_copy(
            scalar.at[plane, pl.ds(0, 8)], field.at[plane, pl.ds(24, 8), whole],
            halo_sems.at[2, plane], halo_sems.at[3, plane],
            device_id=(grp, behind), device_id_type=MESH,
        ))
    for copy in halos:
        copy.start()
    finish, drain = step()()
    finish()

    vel_in = jnp.concatenate([landed[part % HALVES, part // HALVES, :, 0, :] for part in range(OUTER)], 0)
    der_in = jnp.concatenate([landed[part % HALVES, part // HALVES, :, 1, :] for part in range(OUTER)], 0)
    stacked = jnp.concatenate([vel_in.T, (vel_in * weight[...]).T, der_in.T], 0)
    along_y = jnp.dot(stacked, table[...], precision=PRECISE, preferred_element_type=F32)

    def synthesize(kind, component):
        parts = [0.0] * 4
        for digit in range(4):
            start = 128 * kind + (component * 4 + digit) * 16
            cos_re = along_y[start : start + 8, 0:128]
            sin_re = along_y[start : start + 8, 128:256]
            cos_im = along_y[start + 8 : start + 16, 0:128]
            sin_im = along_y[start + 8 : start + 16, 128:256]
            if kind == 1:
                head_re, head_im = -cos_im - sin_re, cos_re - sin_im
            else:
                head_re, head_im = cos_re - sin_im, sin_re + cos_im
            for part in range(4):
                lanes = slice(128 * part, 128 * part + 128)
                tr = turn[0, digit : digit + 1, lanes]
                ti = turn[1, digit : digit + 1, lanes]
                parts[part] = parts[part] + (tr * head_re - ti * head_im)
        return parts

    vel = [synthesize(0, 0), synthesize(0, 1)]
    for component in range(2):
        for part in range(4):
            velocity[component, :, 128 * part : 128 * part + 128] = vel[component][part]
    lift = pltpu.make_async_remote_copy(
        velocity, above, grp_sems.at[0], grp_sems.at[1],
        device_id=(below, blk), device_id_type=MESH,
    )
    lift.start()

    for component in range(2):
        grad_y = synthesize(1, component)
        grad_x = synthesize(2, component)
        adv = [vel[0][a] * grad_x[a] + vel[1][a] * grad_y[a] for a in range(4)]
        even, odd = adv[0] + adv[2], adv[1] + adv[3]
        even_d, odd_d = adv[0] - adv[2], adv[1] - adv[3]
        heads = [(even + odd, None), (even_d, -odd_d), (even - odd, None), (even_d, odd_d)]
        for digit, (p, q) in enumerate(heads):
            tr = turn[0, digit : digit + 1, 0:128]
            ti = turn[1, digit : digit + 1, 0:128]
            if q is None:
                re, im = p * tr, -(p * ti)
            else:
                re, im = p * tr + q * ti, q * tr - p * ti
            start = component * 4 + digit
            pack2[0, pl.ds(start, 8, 16), :] = re
            pack2[1, pl.ds(start, 8, 16), :] = im
            pack2[0, pl.ds(start + 8, 8, 16), :] = im
            pack2[1, pl.ds(start + 8, 8, 16), :] = -re
    forward_y = lax.dot_general(
        table[...], jnp.concatenate([pack2[0], pack2[1]], 1), (((1,), (1,)), ((), ())), precision=PRECISE,
        preferred_element_type=F32,
    )
    for part in range(OUTER):
        sent2[part // HALVES, part % HALVES, :, 0, :] = forward_y[part * INNER : part * INNER + INNER]
    step = exchange(sent2, passed2, landed2, sems2, blk, grp)
    step = step()
    late = (inner == 0) | (inner == INNER - 1)

    def with_halo():
        for copy in own + halos:
            copy.wait()
        lax.fori_loop(0, 4, functools.partial(slopes, field, slope), 0)

    pl.when(jnp.logical_not(late))(with_halo)
    lift.wait_recv()
    refine_along_y(offset, velocity, above, spread, fine_y)

    def transport(plane, carry):
        sections(field, slope, first, fine_y, flow, ready, plane, carry)
        pltpu.make_async_copy(ready.at[plane], out.at[plane], out_sem.at[plane]).start()
        return carry

    done = jnp.where(late, 0, 2)
    lax.fori_loop(0, done, transport, 0)
    finish2, drain2 = step()
    pl.when(late)(with_halo)
    lax.fori_loop(done, 4, transport, 0)
    finish2()

    back = jnp.concatenate([landed2[part % HALVES, part // HALVES, :, 0, :] for part in range(OUTER)], 0)
    along = jnp.dot(back.T, table[...], precision=PRECISE, preferred_element_type=F32)
    heads = []
    for row in range(1, 5):
        start = row * 16
        cos_re = along[start : start + 8, 0:128]
        sin_re = along[start : start + 8, 128:256]
        cos_im = along[start + 8 : start + 16, 0:128]
        sin_im = along[start + 8 : start + 16, 128:256]
        heads.append((cos_re + sin_im, cos_im - sin_re))
    row_index = lax.broadcasted_iota(jnp.int32, (8, 128), 0) % 4 + blk * 4
    row_signed = jnp.where(2 * row_index < NV, row_index, row_index - NV)
    row_wave = row_signed.astype(F32) * (2.0 * np.pi / NV)
    lane = lax.broadcasted_iota(jnp.int32, (8, 128), 1)
    for part in range(4):
        lanes = slice(128 * part, 128 * part + 128)
        re, im = 0.0, 0.0
        for digit, (head_re, head_im) in enumerate(heads):
            tr = turn[0, digit : digit + 1, lanes]
            ti = turn[1, digit : digit + 1, lanes]
            re = re + (tr * head_re + ti * head_im)
            im = im + (tr * head_im - ti * head_re)
        column = lane + 128 * part
        column_signed = column if part < 2 else column - NV
        column_wave = column_signed.astype(F32) * (2.0 * np.pi / NV)
        keep = (3 * jnp.abs(row_signed) < NV) & (3 * jnp.abs(column_signed) < NV)
        gain = jnp.where(keep, TIME_STEP / NV, 0.0)
        damping = jnp.exp(-VISCOSITY * TIME_STEP * (row_wave * row_wave + column_wave * column_wave))
        new_re = damping * (real[:, lanes] - gain * re)
        new_im = damping * (imag[:, lanes] - gain * im)
        for component in range(2):
            rows = slice(4 * component, 4 * component + 4)
            next_coef[component, 0, 0, :, lanes] = new_re[rows]
            next_coef[component, 1, 0, :, lanes] = new_im[rows]
    for plane in range(4):
        pltpu.make_async_copy(ready.at[plane], out.at[plane], out_sem.at[plane]).wait()
    lift.wait_send()
    drain()
    drain2()

def refine_along_y(offset, velocity, above, spread, fine_y):
    for plane in range(4):
        fraction = (offset[plane] % 16).astype(F32) * 0.0625
        for component in range(2):
            mixed = (1.0 - fraction) * velocity[component] + fraction * above[component]
            wide = jnp.concatenate([mixed, mixed[:, :128]], 1)
            rows = jnp.concatenate([wide[:, 128 * m : 128 * m + 256] for m in range(4)], 0)
            top = rows.astype(jnp.bfloat16)
            rest = (rows - top.astype(F32)).astype(jnp.bfloat16)
            fine_y[plane, component] = jnp.dot(
                top, spread[...], preferred_element_type=F32
            ) + jnp.dot(rest, spread[...], preferred_element_type=F32)


def along(values, axis):
    size = values.shape[axis]
    total = 0.0
    for shift, weight in zip((1, 2, 3, 4), STENCIL):
        total = total + (TIME_STEP * 4.0 * weight) * (
            pltpu.roll(values, size - shift, axis) - pltpu.roll(values, shift, axis)
        )
    return total


def slopes(field, slope, plane, carry):
    field[plane, :, 0:PAD] = field[plane, :, NF : NF + PAD]
    field[plane, :, PAD + NF : NF + 2 * PAD] = field[plane, :, PAD : 2 * PAD]
    for m in range(4):
        lanes = slice(SPAN * m, SPAN * m + SPAN)
        window = field[plane, :, SPAN * m : SPAN * m + SPAN + 2 * PAD]
        slope[plane, 0, :, lanes] = along(window[:, PAD : PAD + SPAN], 0)
        slope[plane, 1, :, lanes] = along(window, 1)[:, PAD : PAD + SPAN]
    return carry


def sections(field, slope, first, fine_y, flow, out, plane, carry):
    index = lax.broadcasted_iota(jnp.int32, (8, SPAN), 0)
    share = (index % 4).astype(F32) * 0.25
    half = index < 4
    share_a = jnp.where(half, 1.0 - share, 0.0)
    share_b = jnp.where(half, share, 1.0 - share)
    share_c = jnp.where(half, 0.0, share)
    for m in range(4):
        lanes = slice(SPAN * m, SPAN * m + SPAN)
        inside = slice(PAD + SPAN * m, PAD + SPAN * m + SPAN)
        for tile in range(4):
            rows = slice(8 * tile, 8 * tile + 8)
            speeds = []
            for component in range(2):
                bc = lambda j: jnp.broadcast_to(
                    fine_y[plane, component, 8 * m + j : 8 * m + j + 1, :], (8, SPAN)
                )
                speeds.append(
                    share_a * bc(max(2 * tile - 1, 0))
                    + share_b * bc(2 * tile)
                    + share_c * bc(2 * tile + 1)
                )
                if tile in (1, 2):
                    flow[component, 8 * tile - 8 : 8 * tile, lanes] = speeds[component]
            value = field[plane, rows, inside] - (
                speeds[0] * slope[plane, 0, rows, lanes] + speeds[1] * slope[plane, 1, rows, lanes]
            )
            first[rows, inside] = value
            if m == 0:
                first[rows, PAD + NF : NF + 2 * PAD] = value[:, :PAD]
            if m == 3:
                first[rows, 0:PAD] = value[:, SPAN - PAD :]
    for m in range(4):
        lanes = slice(SPAN * m, SPAN * m + SPAN)
        window = first[:, SPAN * m : SPAN * m + SPAN + 2 * PAD]
        center = window[:, PAD : PAD + SPAN]
        dx = along(center, 0)[8:24]
        dy = along(window[8:24], 1)[:, PAD : PAD + SPAN]
        out[plane, :, lanes] = 0.5 * (
            (field[plane, 8:24, PAD + SPAN * m : PAD + SPAN * m + SPAN] + center[8:24])
            - (flow[0, :, lanes] * dx + flow[1, :, lanes] * dy)
        )
    return carry


def place_kernel(coef, scalar, coef_out, scalar_out, coef_buffer, scalar_buffer, sems):
    routes = [(coef, coef_buffer, coef_out)] + [
        (scalar.at[plane], scalar_buffer.at[plane], scalar_out.at[plane]) for plane in range(4)
    ]
    loads = [pltpu.make_async_copy(a, b, sems.at[0, k]) for k, (a, b, c) in enumerate(routes)]
    stores = [pltpu.make_async_copy(b, c, sems.at[1, k]) for k, (a, b, c) in enumerate(routes)]
    for copy in loads:
        copy.start()
    for load, store in zip(loads, stores):
        load.wait()
        store.start()
    for copy in stores:
        copy.wait()


def spread_table():
    fine = np.arange(512)
    table = np.zeros((256, 512), np.float32)
    table[fine // 4, fine] += 1.0 - (fine % 4) / 4.0
    table[fine // 4 + 1, fine] += (fine % 4) / 4.0
    return table


def vmem():
    return pl.BlockSpec(memory_space=pltpu.VMEM)


def body(velocity_coef, scalar_field, plane_offset):
    table, send, turn, weight = tables()
    dma = pltpu.SemaphoreType.DMA
    anywhere = pl.BlockSpec(memory_space=pl.ANY)
    results = pl.pallas_call(
        step_kernel,
        out_shape=(
            jax.ShapeDtypeStruct(velocity_coef.shape, F32),
            jax.ShapeDtypeStruct(scalar_field.shape, F32),
        ),
        in_specs=[
            pl.BlockSpec(memory_space=pltpu.SMEM), anywhere, anywhere,
            anywhere, anywhere, anywhere, anywhere, anywhere,
        ],
        out_specs=(vmem(), anywhere),
        scratch_shapes=[
            pltpu.VMEM((2, 256, 128), F32),
            pltpu.VMEM((COLUMNS, HALVES, INNER, 2, 128), F32),
            pltpu.VMEM((HALVES, COLUMNS, INNER, 2, 128), F32),
            pltpu.VMEM((HALVES, COLUMNS, INNER, 2, 128), F32),
            pltpu.VMEM((2, 128, 128), F32),
            pltpu.VMEM((COLUMNS, HALVES, INNER, 1, 128), F32),
            pltpu.VMEM((HALVES, COLUMNS, INNER, 1, 128), F32),
            pltpu.VMEM((HALVES, COLUMNS, INNER, 1, 128), F32),
            pltpu.VMEM((2, 8, NV), F32),
            pltpu.VMEM((2, 8, NV), F32),
            pltpu.VMEM((4, 32, NF + 2 * PAD), F32),
            pltpu.VMEM((4, 2, 32, NF), F32),
            pltpu.VMEM((32, NF + 2 * PAD), F32),
            pltpu.VMEM((4, 2, 32, SPAN), F32),
            pltpu.VMEM((2, 16, NF), F32),
            pltpu.VMEM(velocity_coef.shape, F32),
            pltpu.VMEM(table.shape, F32),
            pltpu.VMEM(send.shape, F32),
            pltpu.VMEM(turn.shape, F32),
            pltpu.VMEM(weight.shape, F32),
            pltpu.VMEM((256, 512), jnp.bfloat16),
            pltpu.VMEM(scalar_field.shape, F32),
            dma((3, 4)),
            dma((3, 4)),
            dma((4, 4)),
            dma((2,)),
            dma((4,)),
            dma((6,)),
            dma((4,)),
        ],
        compiler_params=pltpu.CompilerParams(collective_id=0, has_side_effects=True),
        name="step",
    )(
        plane_offset, velocity_coef, scalar_field, jnp.asarray(table), jnp.asarray(send),
        jnp.asarray(turn), jnp.asarray(weight), jnp.asarray(spread_table(), jnp.bfloat16),
    )
    return pl.pallas_call(
        place_kernel,
        out_shape=(
            jax.ShapeDtypeStruct(velocity_coef.shape, F32),
            jax.ShapeDtypeStruct(scalar_field.shape, F32),
        ),
        in_specs=[anywhere, anywhere],
        out_specs=(anywhere, anywhere),
        scratch_shapes=[
            pltpu.VMEM(velocity_coef.shape, F32),
            pltpu.VMEM(scalar_field.shape, F32),
            dma((2, 5)),
        ],
        name="place",
    )(*results)


def solution(mesh):
    in_specs = (P(None, None, "grp", "blk", None), P("grp", "blk", None), P("grp"))
    out_specs = (P(None, None, "grp", "blk", None), P("grp", "blk", None))
    return jax.shard_map(body, mesh=mesh, in_specs=in_specs, out_specs=out_specs, check_vma=False)
```

```python
import functools

import jax
import jax.numpy as jnp
import numpy as np
from jax import lax
from jax.experimental import pallas as pl
from jax.experimental.pallas import tpu as pltpu
from jax.sharding import PartitionSpec as P

TIME_STEP = 0.05
VISCOSITY = 0.5
STENCIL = (0.8, -0.2, 4.0 / 105.0, -1.0 / 280.0)
PRECISE = lax.Precision.HIGH
MESH = pl.DeviceIdType.MESH
NV = 512
OUTER = 8
INNER = 16
COLUMNS, HALVES = 4, 2
BLOCKS = OUTER * INNER
F32 = jnp.float32
PAD = 128
NF = 2048
SPAN = 512


def tables():
    base = np.arange(128)
    angle = 2.0 * np.pi * ((base[:, None] * base[None, :]) % 128) / 128.0
    table = np.concatenate([np.cos(angle), np.sin(angle)], 1)
    wave = np.arange(NV)
    signed = np.where(2 * wave < NV, wave, wave - NV)
    wavenum = 2.0 * np.pi * signed / NV
    rows = np.arange(8) - 1
    ang_x = 2.0 * np.pi * ((rows[:, None] * wave[None, :]) % NV) / NV
    cos_x, sin_x = np.cos(ang_x) / NV, np.sin(ang_x) / NV
    send = np.stack([cos_x, sin_x, -wavenum * sin_x, wavenum * cos_x], 0)
    digit = np.arange(4)
    ang_d = 2.0 * np.pi * ((digit[:, None] * wave[None, :]) % NV) / NV
    turn = np.stack([np.cos(ang_d), np.sin(ang_d)], 0)
    lane_digit = (np.arange(128) // 16) % 4
    ky = 4 * base[:, None] + lane_digit[None, :]
    weight = wavenum[ky]
    as32 = lambda a: np.asarray(a, np.float32)
    return as32(table), as32(send), as32(turn), as32(weight)


def exchange(sent, passed, landed, sems, blk, grp):
    outer, inner = blk // INNER, blk % INNER
    column, half = outer // HALVES, outer % HALVES
    other = 1 - half

    def to_column(there, side, group):
        return pltpu.make_async_remote_copy(
            sent.at[there, side], passed.at[half, column], sems.at[0, group], sems.at[1, group],
            device_id=(grp, (there * HALVES + side) * INNER + inner), device_id_type=MESH,
        )

    def far(k, carry):
        to_column(lax.rem(column + 2 + k, COLUMNS), other, 0).start()
        return carry

    def near(k, carry):
        to_column(lax.rem(column + k, COLUMNS), half, 1).start()
        return carry

    lax.fori_loop(0, COLUMNS, far, 0)
    own = pltpu.make_async_copy(sent.at[column, half], passed.at[half, column], sems.at[2, 0])
    own.start()
    lax.fori_loop(1, COLUMNS, near, 0)

    def arrived(count, group):
        some = pl.ds(0, count)
        return pltpu.make_async_remote_copy(
            passed.at[0, some], passed.at[0, some], sems.at[0, group], sems.at[1, group],
            device_id=(grp, (lax.rem(column + 1, COLUMNS) * HALVES + half) * INNER + inner),
            device_id_type=MESH,
        )

    def spread_inner(side, group):
        mine = pltpu.make_async_copy(
            passed.at[side, :, inner], landed.at[side, :, inner], sems.at[2, group]
        )

        def one(k, carry):
            there = lax.rem(inner + k, INNER)
            pltpu.make_async_remote_copy(
                passed.at[side, :, there], landed.at[side, :, inner],
                sems.at[0, group], sems.at[1, group],
                device_id=(grp, outer * INNER + there), device_id_type=MESH,
            ).start()
            return carry

        lax.fori_loop(1, INNER, one, 0)
        mine.start()
        return mine

    def landed_whole(side, group):
        part = pl.ds(0, INNER - 1)
        return pltpu.make_async_remote_copy(
            passed.at[side, :, part], landed.at[side, :, part], sems.at[0, group], sems.at[1, group],
            device_id=(grp, outer * INNER + lax.rem(inner + 1, INNER)), device_id_type=MESH,
        )

    def pass_near():
        own.wait()
        arrived(COLUMNS - 1, 1).wait_recv()
        mine_near = spread_inner(half, 2)

        def pass_far():
            arrived(COLUMNS, 0).wait_recv()
            mine_far = spread_inner(other, 3)

            def finish():
                mine_near.wait()
                mine_far.wait()
                landed_whole(half, 2).wait_recv()
                landed_whole(other, 3).wait_recv()

            def drain():
                arrived(COLUMNS - 1, 1).wait_send()
                arrived(COLUMNS, 0).wait_send()
                landed_whole(half, 2).wait_send()
                landed_whole(other, 3).wait_send()

            return finish, drain

        return pass_far

    return pass_near


def step_kernel(
    offset, coef_in, scalar, table_in, send_in, turn_in, weight_in, spread_in,
    next_coef, out,
    pack, sent, passed, landed, pack2, sent2, passed2, landed2,
    velocity, above, field, slope, first, fine_y, flow,
    coef, table, send, turn, weight, spread, ready,
    sems, sems2, halo_sems, grp_sems, own_sem, load_sem, out_sem,
):
    blk = lax.axis_index("blk")
    grp = lax.axis_index("grp")
    outer, inner = blk // INNER, blk % INNER
    behind, ahead = lax.rem(blk + BLOCKS - 1, BLOCKS), lax.rem(blk + 1, BLOCKS)
    groups = lax.axis_size("grp")
    below, upper = lax.rem(grp + groups - 1, groups), lax.rem(grp + 1, groups)

    loads = [
        pltpu.make_async_copy(source, target, load_sem.at[k])
        for k, (source, target) in enumerate((
            (coef_in, coef), (send_in, send), (table_in, table),
            (weight_in, weight), (turn_in, turn), (spread_in, spread),
        ))
    ]
    for copy in loads:
        copy.start()

    barrier = pltpu.get_barrier_semaphore()

    def hello(device):
        pl.semaphore_signal(barrier, inc=1, device_id=device, device_id_type=MESH)

    column, side = outer // HALVES, outer % HALVES

    def greet_far(k, carry):
        hello((grp, (lax.rem(column + 2 + k, COLUMNS) * HALVES + 1 - side) * INNER + inner))
        return carry

    def greet_near(k, carry):
        hello((grp, (lax.rem(column + k, COLUMNS) * HALVES + side) * INNER + inner))
        return carry

    def greet_inner(k, carry):
        hello((grp, outer * INNER + lax.rem(inner + k, INNER)))
        return carry

    lax.fori_loop(0, COLUMNS, greet_far, 0)
    hello((grp, behind))
    hello((grp, ahead))
    hello((upper, blk))
    lax.fori_loop(1, COLUMNS, greet_near, 0)
    lax.fori_loop(1, INNER, greet_inner, 0)
    whole = pl.ds(PAD, NF)
    own = [
        pltpu.make_async_copy(
            scalar.at[plane], field.at[plane, pl.ds(8, 16), whole], own_sem.at[plane]
        )
        for plane in range(4)
    ]
    for copy in own:
        copy.start()

    for copy in loads:
        copy.wait()

    real = jnp.concatenate([coef[0, 0, 0], coef[1, 0, 0]], 0)
    imag = jnp.concatenate([coef[0, 1, 0], coef[1, 1, 0]], 0)
    for row in range(8):
        for kind in range(2):
            re, im = 0.0, 0.0
            for digit in range(4):
                lanes = slice(128 * digit, 128 * digit + 128)
                tr = send[2 * kind, row : row + 1, lanes]
                ti = send[2 * kind + 1, row : row + 1, lanes]
                re = re + (tr * real[:, lanes] - ti * imag[:, lanes])
                im = im + (tr * imag[:, lanes] + ti * real[:, lanes])
            start = 128 * kind + row
            pack[0, pl.ds(start, 8, 16), :] = re
            pack[1, pl.ds(start, 8, 16), :] = -im
            pack[0, pl.ds(start + 8, 8, 16), :] = im
            pack[1, pl.ds(start + 8, 8, 16), :] = re
    along_x = lax.dot_general(
        table[...], jnp.concatenate([pack[0], pack[1]], 1), (((1,), (1,)), ((), ())), precision=PRECISE,
        preferred_element_type=F32,
    )
    for part in range(OUTER):
        rows = slice(part * INNER, part * INNER + INNER)
        sent[part // HALVES, part % HALVES, :, 0, :] = along_x[rows, 0:128]
        sent[part // HALVES, part % HALVES, :, 1, :] = along_x[rows, 128:256]

    pl.semaphore_wait(barrier, OUTER - 1 + INNER - 1 + 3)

    step = exchange(sent, passed, landed, sems, blk, grp)
    halos = []
    for plane in range(4):
        halos.append(pltpu.make_async_remote_copy(
            scalar.at[plane, pl.ds(8, 8)], field.at[plane, pl.ds(0, 8), whole],
            halo_sems.at[0, plane], halo_sems.at[1, plane],
            device_id=(grp, ahead), device_id_type=MESH,
        ))
        halos.append(pltpu.make_async_remote_copy(
            scalar.at[plane, pl.ds(0, 8)], field.at[plane, pl.ds(24, 8), whole],
            halo_sems.at[2, plane], halo_sems.at[3, plane],
            device_id=(grp, behind), device_id_type=MESH,
        ))
    for copy in halos:
        copy.start()
    finish, drain = step()()
    finish()

    vel_in = jnp.concatenate([landed[part % HALVES, part // HALVES, :, 0, :] for part in range(OUTER)], 0)
    der_in = jnp.concatenate([landed[part % HALVES, part // HALVES, :, 1, :] for part in range(OUTER)], 0)
    stacked = jnp.concatenate([vel_in.T, (vel_in * weight[...]).T, der_in.T], 0)
    along_y = jnp.dot(stacked, table[...], precision=PRECISE, preferred_element_type=F32)

    def synthesize(kind, component):
        parts = [0.0] * 4
        for digit in range(4):
            start = 128 * kind + (component * 4 + digit) * 16
            cos_re = along_y[start : start + 8, 0:128]
            sin_re = along_y[start : start + 8, 128:256]
            cos_im = along_y[start + 8 : start + 16, 0:128]
            sin_im = along_y[start + 8 : start + 16, 128:256]
            if kind == 1:
                head_re, head_im = -cos_im - sin_re, cos_re - sin_im
            else:
                head_re, head_im = cos_re - sin_im, sin_re + cos_im
            for part in range(4):
                lanes = slice(128 * part, 128 * part + 128)
                tr = turn[0, digit : digit + 1, lanes]
                ti = turn[1, digit : digit + 1, lanes]
                parts[part] = parts[part] + (tr * head_re - ti * head_im)
        return parts

    vel = [synthesize(0, 0), synthesize(0, 1)]
    for component in range(2):
        for part in range(4):
            velocity[component, :, 128 * part : 128 * part + 128] = vel[component][part]
    lift = pltpu.make_async_remote_copy(
        velocity, above, grp_sems.at[0], grp_sems.at[1],
        device_id=(below, blk), device_id_type=MESH,
    )
    lift.start()

    for component in range(2):
        grad_y = synthesize(1, component)
        grad_x = synthesize(2, component)
        adv = [vel[0][a] * grad_x[a] + vel[1][a] * grad_y[a] for a in range(4)]
        even, odd = adv[0] + adv[2], adv[1] + adv[3]
        even_d, odd_d = adv[0] - adv[2], adv[1] - adv[3]
        heads = [(even + odd, None), (even_d, -odd_d), (even - odd, None), (even_d, odd_d)]
        for digit, (p, q) in enumerate(heads):
            tr = turn[0, digit : digit + 1, 0:128]
            ti = turn[1, digit : digit + 1, 0:128]
            if q is None:
                re, im = p * tr, -(p * ti)
            else:
                re, im = p * tr + q * ti, q * tr - p * ti
            start = component * 4 + digit
            pack2[0, pl.ds(start, 8, 16), :] = re
            pack2[1, pl.ds(start, 8, 16), :] = im
            pack2[0, pl.ds(start + 8, 8, 16), :] = im
            pack2[1, pl.ds(start + 8, 8, 16), :] = -re
    forward_y = lax.dot_general(
        table[...], jnp.concatenate([pack2[0], pack2[1]], 1), (((1,), (1,)), ((), ())), precision=PRECISE,
        preferred_element_type=F32,
    )
    for part in range(OUTER):
        sent2[part // HALVES, part % HALVES, :, 0, :] = forward_y[part * INNER : part * INNER + INNER]
    step = exchange(sent2, passed2, landed2, sems2, blk, grp)
    step = step()
    late = (inner == 0) | (inner == INNER - 1)

    def with_halo():
        for copy in own + halos:
            copy.wait()
        lax.fori_loop(0, 4, functools.partial(slopes, field, slope), 0)

    pl.when(jnp.logical_not(late))(with_halo)
    lift.wait_recv()
    refine_along_y(offset, velocity, above, spread, fine_y)

    def transport(plane, carry):
        sections(field, slope, first, fine_y, flow, ready, plane, carry)
        pltpu.make_async_copy(ready.at[plane], out.at[plane], out_sem.at[plane]).start()
        return carry

    done = jnp.where(late, 0, 2)
    lax.fori_loop(0, done, transport, 0)
    finish2, drain2 = step()
    pl.when(late)(with_halo)
    lax.fori_loop(done, 4, transport, 0)
    finish2()

    back = jnp.concatenate([landed2[part % HALVES, part // HALVES, :, 0, :] for part in range(OUTER)], 0)
    along = jnp.dot(back.T, table[...], precision=PRECISE, preferred_element_type=F32)
    heads = []
    for row in range(1, 5):
        start = row * 16
        cos_re = along[start : start + 8, 0:128]
        sin_re = along[start : start + 8, 128:256]
        cos_im = along[start + 8 : start + 16, 0:128]
        sin_im = along[start + 8 : start + 16, 128:256]
        heads.append((cos_re + sin_im, cos_im - sin_re))
    row_index = lax.broadcasted_iota(jnp.int32, (8, 128), 0) % 4 + blk * 4
    row_signed = jnp.where(2 * row_index < NV, row_index, row_index - NV)
    row_wave = row_signed.astype(F32) * (2.0 * np.pi / NV)
    lane = lax.broadcasted_iota(jnp.int32, (8, 128), 1)
    for part in range(4):
        lanes = slice(128 * part, 128 * part + 128)
        re, im = 0.0, 0.0
        for digit, (head_re, head_im) in enumerate(heads):
            tr = turn[0, digit : digit + 1, lanes]
            ti = turn[1, digit : digit + 1, lanes]
            re = re + (tr * head_re + ti * head_im)
            im = im + (tr * head_im - ti * head_re)
        column = lane + 128 * part
        column_signed = column if part < 2 else column - NV
        column_wave = column_signed.astype(F32) * (2.0 * np.pi / NV)
        keep = (3 * jnp.abs(row_signed) < NV) & (3 * jnp.abs(column_signed) < NV)
        gain = jnp.where(keep, TIME_STEP / NV, 0.0)
        damping = jnp.exp(-VISCOSITY * TIME_STEP * (row_wave * row_wave + column_wave * column_wave))
        new_re = damping * (real[:, lanes] - gain * re)
        new_im = damping * (imag[:, lanes] - gain * im)
        for component in range(2):
            rows = slice(4 * component, 4 * component + 4)
            next_coef[component, 0, 0, :, lanes] = new_re[rows]
            next_coef[component, 1, 0, :, lanes] = new_im[rows]
    for plane in range(4):
        pltpu.make_async_copy(ready.at[plane], out.at[plane], out_sem.at[plane]).wait()
    lift.wait_send()
    drain()
    drain2()

def refine_along_y(offset, velocity, above, spread, fine_y):
    for plane in range(4):
        fraction = (offset[plane] % 16).astype(F32) * 0.0625
        for component in range(2):
            mixed = (1.0 - fraction) * velocity[component] + fraction * above[component]
            wide = jnp.concatenate([mixed, mixed[:, :128]], 1)
            rows = jnp.concatenate([wide[:, 128 * m : 128 * m + 256] for m in range(4)], 0)
            top = rows.astype(jnp.bfloat16)
            rest = (rows - top.astype(F32)).astype(jnp.bfloat16)
            fine_y[plane, component] = jnp.dot(
                top, spread[...], preferred_element_type=F32
            ) + jnp.dot(rest, spread[...], preferred_element_type=F32)


def along(values, axis):
    size = values.shape[axis]
    total = 0.0
    for shift, weight in zip((1, 2, 3, 4), STENCIL):
        total = total + (TIME_STEP * 4.0 * weight) * (
            pltpu.roll(values, size - shift, axis) - pltpu.roll(values, shift, axis)
        )
    return total


def slopes(field, slope, plane, carry):
    field[plane, :, 0:PAD] = field[plane, :, NF : NF + PAD]
    field[plane, :, PAD + NF : NF + 2 * PAD] = field[plane, :, PAD : 2 * PAD]
    for m in range(4):
        lanes = slice(SPAN * m, SPAN * m + SPAN)
        window = field[plane, :, SPAN * m : SPAN * m + SPAN + 2 * PAD]
        slope[plane, 0, :, lanes] = along(window[:, PAD : PAD + SPAN], 0)
        slope[plane, 1, :, lanes] = along(window, 1)[:, PAD : PAD + SPAN]
    return carry


def sections(field, slope, first, fine_y, flow, out, plane, carry):
    index = lax.broadcasted_iota(jnp.int32, (8, SPAN), 0)
    share = (index % 4).astype(F32) * 0.25
    half = index < 4
    share_a = jnp.where(half, 1.0 - share, 0.0)
    share_b = jnp.where(half, share, 1.0 - share)
    share_c = jnp.where(half, 0.0, share)
    for m in range(4):
        lanes = slice(SPAN * m, SPAN * m + SPAN)
        inside = slice(PAD + SPAN * m, PAD + SPAN * m + SPAN)
        for tile in range(4):
            rows = slice(8 * tile, 8 * tile + 8)
            speeds = []
            for component in range(2):
                bc = lambda j: jnp.broadcast_to(
                    fine_y[plane, component, 8 * m + j : 8 * m + j + 1, :], (8, SPAN)
                )
                speeds.append(
                    share_a * bc(max(2 * tile - 1, 0))
                    + share_b * bc(2 * tile)
                    + share_c * bc(2 * tile + 1)
                )
                if tile in (1, 2):
                    flow[component, 8 * tile - 8 : 8 * tile, lanes] = speeds[component]
            value = field[plane, rows, inside] - (
                speeds[0] * slope[plane, 0, rows, lanes] + speeds[1] * slope[plane, 1, rows, lanes]
            )
            first[rows, inside] = value
            if m == 0:
                first[rows, PAD + NF : NF + 2 * PAD] = value[:, :PAD]
            if m == 3:
                first[rows, 0:PAD] = value[:, SPAN - PAD :]
    for m in range(4):
        lanes = slice(SPAN * m, SPAN * m + SPAN)
        window = first[:, SPAN * m : SPAN * m + SPAN + 2 * PAD]
        center = window[:, PAD : PAD + SPAN]
        dx = along(center, 0)[8:24]
        dy = along(window[8:24], 1)[:, PAD : PAD + SPAN]
        out[plane, :, lanes] = 0.5 * (
            (field[plane, 8:24, PAD + SPAN * m : PAD + SPAN * m + SPAN] + center[8:24])
            - (flow[0, :, lanes] * dx + flow[1, :, lanes] * dy)
        )
    return carry


def place_kernel(coef, scalar, coef_out, scalar_out, sems):
    stores = [pltpu.make_async_copy(coef, coef_out, sems.at[4])] + [
        pltpu.make_async_copy(scalar.at[plane], scalar_out.at[plane], sems.at[plane])
        for plane in range(4)
    ]
    for copy in stores:
        copy.start()
    for copy in stores:
        copy.wait()


def spread_table():
    fine = np.arange(512)
    table = np.zeros((256, 512), np.float32)
    table[fine // 4, fine] += 1.0 - (fine % 4) / 4.0
    table[fine // 4 + 1, fine] += (fine % 4) / 4.0
    return table


def vmem():
    return pl.BlockSpec(memory_space=pltpu.VMEM)


def body(velocity_coef, scalar_field, plane_offset):
    table, send, turn, weight = tables()
    dma = pltpu.SemaphoreType.DMA
    anywhere = pl.BlockSpec(memory_space=pl.ANY)
    results = pl.pallas_call(
        step_kernel,
        out_shape=(
            jax.ShapeDtypeStruct(velocity_coef.shape, F32),
            jax.ShapeDtypeStruct(scalar_field.shape, F32),
        ),
        in_specs=[
            pl.BlockSpec(memory_space=pltpu.SMEM), *[pl.BlockSpec(memory_space=pltpu.HBM)] * 7,
        ],
        out_specs=(vmem(), anywhere),
        scratch_shapes=[
            pltpu.VMEM((2, 256, 128), F32),
            pltpu.VMEM((COLUMNS, HALVES, INNER, 2, 128), F32),
            pltpu.VMEM((HALVES, COLUMNS, INNER, 2, 128), F32),
            pltpu.VMEM((HALVES, COLUMNS, INNER, 2, 128), F32),
            pltpu.VMEM((2, 128, 128), F32),
            pltpu.VMEM((COLUMNS, HALVES, INNER, 1, 128), F32),
            pltpu.VMEM((HALVES, COLUMNS, INNER, 1, 128), F32),
            pltpu.VMEM((HALVES, COLUMNS, INNER, 1, 128), F32),
            pltpu.VMEM((2, 8, NV), F32),
            pltpu.VMEM((2, 8, NV), F32),
            pltpu.VMEM((4, 32, NF + 2 * PAD), F32),
            pltpu.VMEM((4, 2, 32, NF), F32),
            pltpu.VMEM((32, NF + 2 * PAD), F32),
            pltpu.VMEM((4, 2, 32, SPAN), F32),
            pltpu.VMEM((2, 16, NF), F32),
            pltpu.VMEM(velocity_coef.shape, F32),
            pltpu.VMEM(table.shape, F32),
            pltpu.VMEM(send.shape, F32),
            pltpu.VMEM(turn.shape, F32),
            pltpu.VMEM(weight.shape, F32),
            pltpu.VMEM((256, 512), jnp.bfloat16),
            pltpu.VMEM(scalar_field.shape, F32),
            dma((3, 4)),
            dma((3, 4)),
            dma((4, 4)),
            dma((2,)),
            dma((4,)),
            dma((6,)),
            dma((4,)),
        ],
        compiler_params=pltpu.CompilerParams(
            collective_id=0, has_side_effects=True, vmem_limit_bytes=12 << 20
        ),
        name="step",
    )(
        plane_offset, *[
            pltpu.with_memory_space_constraint(array, pltpu.HBM)
            for array in (
                velocity_coef, scalar_field, jnp.asarray(table), jnp.asarray(send),
                jnp.asarray(turn), jnp.asarray(weight), jnp.asarray(spread_table(), jnp.bfloat16),
            )
        ],
    )
    return pl.pallas_call(
        place_kernel,
        out_shape=(
            jax.ShapeDtypeStruct(velocity_coef.shape, F32),
            jax.ShapeDtypeStruct(scalar_field.shape, F32),
        ),
        in_specs=[anywhere, anywhere],
        out_specs=(anywhere, anywhere),
        scratch_shapes=[dma((5,))],
        compiler_params=pltpu.CompilerParams(vmem_limit_bytes=4 << 20),
        name="place",
    )(*results)


def solution(mesh):
    in_specs = (P(None, None, "grp", "blk", None), P("grp", "blk", None), P("grp"))
    out_specs = (P(None, None, "grp", "blk", None), P("grp", "blk", None))
    return jax.shard_map(body, mesh=mesh, in_specs=in_specs, out_specs=out_specs, check_vma=False)
```
